32 devices in a mesh: img: 4 (over x, core), seq: 2 (over y), tp: 4 (over z).
Axes of the slice: x: 2, y: 2, z: 4, core: 2. Of those that a mesh axis runs over, the one named last changes fastest.
Arguments:
- vit_qkv: bfloat16 [4, 512, 3, 1280], P('img', ('seq', 'tp')), may hold values from -6 to 6
- patch_counts: int32 [4], P('img'), may hold values from 128 to 512, as said below
- vit_out_weight: bfloat16 [1280, 1280], replicated, may hold values from -0.15625 to 0.15625
- vit_norm_gain: float32 [1280], replicated, may hold values from 0.25 to 1.75
- merger_weight: bfloat16 [5120, 8192], P(('img', 'seq'), 'tp'), may hold values from -8 to 8
- lm_norm_gain: float32 [8192], P('tp'), may hold values from 0.25 to 1.75
- kv_weight: bfloat16 [8192, 2048], P('tp', ('img', 'seq')), may hold values from -0.0625 to 0.0625
- queries: bfloat16 [4, 1024, 64, 128], P('img', 'seq', 'tp'), may hold values from -6 to 6
- span_kv: bfloat16 [4, 1024, 2, 8, 128], P('img', 'seq', None, 'tp'), may hold values from -6 to 6
Outputs:
- lm_attention: bfloat16 [4, 1024, 64, 128], P('img', 'seq', 'tp')
The draws below stay inside these ranges and needn't reach their ends.
Inputs may be any that keep to these rules, and one draw needn't show every extreme that they name: `patch_counts`: each count is a multiple of 4, at least 128, and some image has exactly 512.
All inputs are finite; a program needn't handle non-finite values.
Results may differ from the reference program's by a relative error of at most 0.04.
Values may be sent and summed in bfloat16 or wider, within the bound.
No kernel may reach another device: no remote copies, remote signals or barrier semaphores. Data moves between devices by JAX's collectives and lax.ppermute only.
A program may use at most 128 MiB of HBM per device.

```python
import math
import jax
import jax.numpy as jnp
from jax import lax

VIT_D = 1280
VIT_HEADS = 16
VIT_HDIM = 80
D = 8192
HQ = 64
KVH = 8
HD = 128
SPAN = 512
IMAGES = 4
PATCHES = 512
VIS = 128
TOKS = 1024
N_SEQ = 2


def draw_patch_counts(key, part):
    count_key, pick_key = jax.random.split(jax.random.fold_in(key, 11))
    counts = jax.random.randint(count_key, (IMAGES,), PATCHES // 16, PATCHES // 4 + 1) * 4
    chosen = jax.random.randint(pick_key, (), 0, IMAGES)
    return jnp.where(jnp.arange(IMAGES) == chosen, PATCHES, counts).astype(jnp.int32)


def base_field(key, shape):
    return jnp.clip(jax.random.normal(key, shape, jnp.float32), -6.0, 6.0)


def score_levels():
    return (110.0, 190.0, 290.0)


def plant_plan(level_key, target, head_size):
    parts = jax.random.split(level_key, 3)
    sign_vector = jnp.where(jax.random.bernoulli(parts[0], 0.5, (head_size,)), 1.0, -1.0).astype(jnp.float32)
    score_gap = jax.random.uniform(parts[1], (), jnp.float32, 1.0, 3.0)
    strength = min(math.sqrt(target / math.sqrt(head_size)), 5.9)
    top_score = strength * strength * math.sqrt(head_size)
    second_strength = strength * (top_score - score_gap) / top_score
    return (sign_vector, strength, second_strength, parts[2])


def draw_vit_qkv(key, part):
    base_key, plant_key = jax.random.split(jax.random.fold_in(key, 31))
    values = base_field(base_key, (IMAGES, PATCHES, 3, VIT_D))
    usable = PATCHES // 4
    for image_index in range(IMAGES):
        for level_index, target in enumerate(score_levels()):
            level_key = jax.random.fold_in(plant_key, image_index * 8 + level_index)
            sign_vector, strength, second_strength, pick_key = plant_plan(level_key, target, VIT_HDIM)
            picks = jax.random.split(pick_key, 4)
            query_slot = jax.random.randint(picks[0], (), 0, usable).astype(jnp.int32)
            first_slot = jax.random.randint(picks[1], (), 0, usable).astype(jnp.int32)
            second_slot = ((first_slot + 1 + jax.random.randint(picks[2], (), 0, usable - 1)) % usable).astype(jnp.int32)
            head_start = (jax.random.randint(picks[3], (), 0, VIT_HEADS) * VIT_HDIM).astype(jnp.int32)
            image_id = jnp.int32(image_index)
            values = lax.dynamic_update_slice(values, (strength * sign_vector).reshape(1, 1, 1, VIT_HDIM), (image_id, query_slot, jnp.int32(0), head_start))
            values = lax.dynamic_update_slice(values, (strength * sign_vector).reshape(1, 1, 1, VIT_HDIM), (image_id, first_slot, jnp.int32(1), head_start))
            values = lax.dynamic_update_slice(values, (second_strength * sign_vector).reshape(1, 1, 1, VIT_HDIM), (image_id, second_slot, jnp.int32(1), head_start))
    return values.astype(jnp.bfloat16)


def draw_merger_weight(key, part):
    rows_total = 4 * VIT_D
    parts = jax.random.split(jax.random.fold_in(key, 53), 2)
    column_place = jnp.arange(D, dtype=jnp.float32) / D
    jitter = jnp.exp(jax.random.uniform(parts[1], (D,), jnp.float32, -0.69, 0.69))
    column_scale = jnp.power(10.0, column_place) * jitter
    values = jax.random.normal(parts[0], (rows_total, D), jnp.float32) * rows_total ** (-0.5) * column_scale[None, :]
    return jnp.clip(values, -8.0, 8.0).astype(jnp.bfloat16)


def lm_plants(key):
    plans = []
    for image_index in range(IMAGES):
        for level_index, target in enumerate(score_levels()):
            level_key = jax.random.fold_in(key, image_index * 8 + level_index)
            sign_vector, strength, second_strength, pick_key = plant_plan(level_key, target, HD)
            picks = jax.random.split(pick_key, 5)
            sample_index = jax.random.randint(picks[0], (), 0, TOKS // SPAN)
            position = jax.random.randint(picks[1], (), SPAN // 2, SPAN)
            first_place = jax.random.randint(picks[2], (), 0, position + 1)
            second_place = (first_place + 1 + jax.random.randint(picks[3], (), 0, position)) % (position + 1)
            head_index = jax.random.randint(picks[4], (), 0, HQ).astype(jnp.int32)
            start = sample_index * SPAN
            plans.append((image_index, (start + position).astype(jnp.int32), (start + first_place).astype(jnp.int32), (start + second_place).astype(jnp.int32), head_index, sign_vector, strength, second_strength))
    return plans


def draw_queries(key, part):
    values = base_field(jax.random.fold_in(key, 41), (IMAGES, TOKS, HQ, HD))
    for image_index, query_token, first_token, second_token, head_index, sign_vector, strength, second_strength in lm_plants(jax.random.fold_in(key, 61)):
        values = lax.dynamic_update_slice(values, (strength * sign_vector).reshape(1, 1, 1, HD), (jnp.int32(image_index), query_token, head_index, jnp.int32(0)))
    return values.astype(jnp.bfloat16)


def draw_span_kv(key, part):
    values = base_field(jax.random.fold_in(key, 43), (IMAGES, TOKS, 2, KVH, HD))
    for image_index, query_token, first_token, second_token, head_index, sign_vector, strength, second_strength in lm_plants(jax.random.fold_in(key, 61)):
        kv_head = (head_index // (HQ // KVH)).astype(jnp.int32)
        image_id = jnp.int32(image_index)
        values = lax.dynamic_update_slice(values, (strength * sign_vector).reshape(1, 1, 1, 1, HD), (image_id, first_token, jnp.int32(0), kv_head, jnp.int32(0)))
        values = lax.dynamic_update_slice(values, (second_strength * sign_vector).reshape(1, 1, 1, 1, HD), (image_id, second_token, jnp.int32(0), kv_head, jnp.int32(0)))
    return values.astype(jnp.bfloat16)


def levels(stream_key, shape, cuts, low, largest):
    factor_of, own = 1.0, jax.random.fold_in(stream_key, 6)
    for dim, blocks in cuts:
        heights = jnp.exp(jax.random.uniform(jax.random.fold_in(own, dim), (blocks,), jnp.float32, low / len(cuts), largest / len(cuts)))
        factor_of = factor_of * jnp.repeat(heights, shape[dim] // blocks).reshape([-1 if axis == dim else 1 for axis in range(len(shape))])
    return factor_of


def normal_values(own_key, extent, deviation, most, pieces=(), held_as=jnp.bfloat16):
    drawn = deviation * jax.random.normal(own_key, extent, jnp.float32)
    if pieces:
        drawn = drawn * levels(own_key, extent, pieces, -0.22, 0.18)
    return jnp.clip(drawn, -most, most).astype(held_as)


def setup_inputs(seed: int = 0) -> dict:
    key_of = jax.random.split(jax.random.key(seed), 10)
    return {
        "vit_qkv": draw_vit_qkv(jax.random.fold_in(key_of[9], 71), 0),
        "patch_counts": draw_patch_counts(jax.random.fold_in(key_of[9], 71), 0),
        "vit_out_weight": normal_values(key_of[2], (VIT_D, VIT_D), VIT_D ** -0.5, 0.15625),
        "vit_norm_gain": jnp.clip(1.0 + 0.15 * jax.random.normal(key_of[3], (VIT_D,), jnp.float32), 0.25, 1.75),
        "merger_weight": draw_merger_weight(jax.random.fold_in(key_of[9], 71), 0),
        "lm_norm_gain": jnp.clip(1.0 + 0.15 * jax.random.normal(key_of[5], (D,), jnp.float32), 0.25, 1.75),
        "kv_weight": normal_values(key_of[6], (D, 2 * KVH * HD), D ** -0.5, 0.0625, ((0, 4), (1, 8))),
        "queries": draw_queries(jax.random.fold_in(key_of[9], 71), 0),
        "span_kv": draw_span_kv(jax.random.fold_in(key_of[9], 71), 0),
    }


masked_score = -1e+30

def vit_image(qkv_rows, patch_total, out_weight, norm_gain):
    slots = qkv_rows.shape[0]
    query_rows = qkv_rows[:, 0].reshape(slots, VIT_HEADS, VIT_HDIM).astype(jnp.float32)
    key_rows = qkv_rows[:, 1].reshape(slots, VIT_HEADS, VIT_HDIM).astype(jnp.float32)
    value_rows = qkv_rows[:, 2].reshape(slots, VIT_HEADS, VIT_HDIM).astype(jnp.float32)
    usable = jnp.arange(slots, dtype=jnp.int32) < patch_total
    block_rows = math.gcd(slots, 512)
    scaling = VIT_HDIM ** (-0.5)

    def attend(query_block):
        scores = jnp.einsum('qhd,khd->hqk', query_block, key_rows) * scaling
        scores = jnp.where(usable[None, None, :], scores, masked_score)
        peak = lax.optimization_barrier(jnp.max(scores, axis=-1, keepdims=True))
        weights = jnp.where(usable[None, None, :], jnp.exp(scores - peak), 0.0)
        weight_sum = lax.optimization_barrier(jnp.sum(weights, axis=-1))
        blended = jnp.einsum('hqk,khd->hqd', weights.astype(jnp.bfloat16).astype(jnp.float32), value_rows)
        return jnp.transpose(blended / weight_sum[..., None], (1, 0, 2))
    attended = lax.map(attend, query_rows.reshape(slots // block_rows, block_rows, VIT_HEADS, VIT_HDIM))
    attended = attended.reshape(slots, VIT_D).astype(jnp.bfloat16)
    hidden = jnp.dot(attended, out_weight, preferred_element_type=jnp.float32)
    hidden = jnp.where(usable[:, None], hidden, 0.0)
    centred = hidden - lax.optimization_barrier(jnp.mean(hidden, axis=-1, keepdims=True))
    spread = lax.optimization_barrier(jnp.mean(centred * centred, axis=-1, keepdims=True))
    normed = (centred * lax.rsqrt(spread + 1e-06) * norm_gain).astype(jnp.bfloat16)
    return normed.reshape(slots // 4, 4 * VIT_D)

def lm_image(query_rows, span_rows, visual_kv, visual_total):
    groups = HQ // KVH
    scaling = HD ** (-0.5)
    vis_keys = visual_kv[:, 0].astype(jnp.float32)
    vis_values = visual_kv[:, 1].astype(jnp.float32)
    usable = jnp.arange(VIS, dtype=jnp.int32) < visual_total
    causal = jnp.arange(SPAN)[:, None] >= jnp.arange(SPAN)[None, :]

    def sample(inputs):
        sample_queries, sample_span = inputs
        grouped = sample_queries.reshape(SPAN, KVH, groups, HD).astype(jnp.float32)
        far_scores = jnp.einsum('ckgd,nkd->kgcn', grouped, vis_keys) * scaling
        far_scores = jnp.where(usable[None, None, None, :], far_scores, masked_score)
        near_keys = sample_span[:, 0].astype(jnp.float32)
        near_values = sample_span[:, 1].astype(jnp.float32)
        near_scores = jnp.einsum('ckgd,nkd->kgcn', grouped, near_keys) * scaling
        near_scores = jnp.where(causal[None, None], near_scores, masked_score)
        peak = jnp.maximum(lax.optimization_barrier(jnp.max(far_scores, axis=-1)), lax.optimization_barrier(jnp.max(near_scores, axis=-1)))
        far_weights = jnp.where(usable[None, None, None, :], jnp.exp(far_scores - peak[..., None]), 0.0)
        near_weights = jnp.where(causal[None, None], jnp.exp(near_scores - peak[..., None]), 0.0)
        weight_sum = lax.optimization_barrier(jnp.sum(far_weights, axis=-1)) + lax.optimization_barrier(jnp.sum(near_weights, axis=-1))
        blended = jnp.einsum('kgcn,nkd->kgcd', far_weights.astype(jnp.bfloat16).astype(jnp.float32), vis_values)
        blended = blended + jnp.einsum('kgcn,nkd->kgcd', near_weights.astype(jnp.bfloat16).astype(jnp.float32), near_values)
        result = jnp.transpose(blended / weight_sum[..., None], (2, 0, 1, 3))
        return result.reshape(SPAN, HQ, HD).astype(jnp.bfloat16)
    result = lax.map(sample, (query_rows.reshape(N_SEQ, SPAN, HQ, HD), span_rows.reshape(N_SEQ, SPAN, 2, KVH, HD)))
    return result.reshape(TOKS, HQ, HD)

def reference(vit_qkv, patch_counts, vit_out_weight, vit_norm_gain, merger_weight, lm_norm_gain, kv_weight, queries, span_kv):

    def per_image(inputs):
        qkv_rows, patch_total, query_rows, span_rows = inputs
        merged = vit_image(qkv_rows, patch_total, vit_out_weight, vit_norm_gain)
        embedded = jnp.dot(merged, merger_weight, preferred_element_type=jnp.float32).astype(jnp.bfloat16)
        embedded_wide = lax.optimization_barrier(embedded).astype(jnp.float32)
        square_mean = lax.optimization_barrier(jnp.mean(embedded_wide * embedded_wide, axis=-1, keepdims=True))
        lm_normed = (embedded_wide * lax.rsqrt(square_mean + 1e-06) * lm_norm_gain).astype(jnp.bfloat16)
        visual_kv = jnp.dot(lm_normed, kv_weight, preferred_element_type=jnp.float32).astype(jnp.bfloat16)
        visual_kv = visual_kv.reshape(VIS, 2, KVH, HD)
        return lm_image(query_rows, span_rows, visual_kv, patch_total // 4)
    return lax.map(per_image, (vit_qkv, patch_counts, queries, span_kv))
```

```python
import jax
import jax.numpy as jnp
from jax import lax
from jax.sharding import Mesh
from jax.sharding import PartitionSpec as P

VIT_D = 1280
VIT_HEADS = 16
VIT_HDIM = 80
D = 8192
HQ = 64
KVH = 8
HD = 128


masked_score = -1e30


def fold_block(running, scores, usable, value_block, forms):
    peak, weight_sum, blended = running
    scores = jnp.where(usable, scores, masked_score)
    new_peak = jnp.maximum(peak, jnp.max(scores, axis=-1))
    weights = jnp.where(usable, jnp.exp(scores - new_peak[..., None]), 0.0)
    decay = jnp.exp(peak - new_peak)
    weight_sum = weight_sum * decay + jnp.sum(weights, axis=-1)
    blended = blended * decay[..., None] + jnp.einsum(
        forms, weights.astype(jnp.bfloat16), value_block, preferred_element_type=jnp.float32
    )
    return (new_peak, weight_sum, blended)


def local(
    vit_qkv,
    patch_counts,
    vit_out_weight,
    vit_norm_gain,
    merger_weight,
    lm_norm_gain,
    kv_weight,
    queries,
    span_kv,
):
    patch_rows = vit_qkv.shape[1]
    tp_count = lax.axis_size("tp")
    seq_index = lax.axis_index("seq")
    tp_index = lax.axis_index("tp")
    patch_total = patch_counts[0]
    local_qkv = vit_qkv[0].reshape(patch_rows, 3, VIT_HEADS, VIT_HDIM)
    scaling = VIT_HDIM ** (-0.5)
    spread = lax.all_to_all(local_qkv, "seq", split_axis=2, concat_axis=0, tiled=True)
    local_rows = spread.shape[0]

    def seq_rows(index):
        source = index // local_rows
        within = index % local_rows
        return (within // patch_rows * tp_count + source) * patch_rows + within % patch_rows

    heads_local = spread.shape[2]
    query_count = spread.shape[0]
    query_rows = spread[:, 0]
    running = (
        jnp.full((heads_local, query_count), masked_score, jnp.float32),
        jnp.zeros((heads_local, query_count), jnp.float32),
        jnp.zeros((heads_local, query_count, VIT_HDIM), jnp.float32),
    )
    make_heads_local = query_rows.shape[1]
    key_piece = lax.all_gather(spread[:, 1], "tp", axis=0, tiled=True)
    value_piece = lax.all_gather(spread[:, 2], "tp", axis=0, tiled=True)
    blocks = key_piece.shape[0] // local_rows
    key_blocks = key_piece.reshape(blocks, local_rows, make_heads_local, VIT_HDIM)
    value_blocks = value_piece.reshape(blocks, local_rows, make_heads_local, VIT_HDIM)
    offsets = jnp.arange(blocks, dtype=jnp.int32) * local_rows

    def make_advance(state, inputs):
        key_block, value_block, offset = inputs
        usable = seq_rows(offset + jnp.arange(local_rows, dtype=jnp.int32)) < patch_total
        scores = (
            jnp.einsum("qhd,khd->hqk", query_rows, key_block, preferred_element_type=jnp.float32)
            * scaling
        )
        return (fold_block(state, scores, usable[None, None, :], value_block, "hqk,khd->hqd"), None)

    result, _ = lax.scan(make_advance, running, (key_blocks, value_blocks, offsets))
    state = result
    peak, weight_sum, blended = state
    returned = lax.all_to_all(
        jnp.transpose(blended / weight_sum[..., None], (1, 0, 2)).astype(jnp.bfloat16),
        "seq",
        split_axis=0,
        concat_axis=1,
        tiled=True,
    )
    attended = returned.reshape(patch_rows, VIT_D)
    hidden = jnp.dot(attended, vit_out_weight, preferred_element_type=jnp.float32)
    patch_ids = (seq_index * tp_count + tp_index) * patch_rows + jnp.arange(
        patch_rows, dtype=jnp.int32
    )
    hidden = jnp.where((patch_ids < patch_total)[:, None], hidden, 0.0)
    centred = hidden - jnp.mean(hidden, axis=-1, keepdims=True)
    spread_sq = jnp.mean(centred * centred, axis=-1, keepdims=True)
    normed = (centred * lax.rsqrt(spread_sq + 1e-06) * vit_norm_gain).astype(jnp.bfloat16)
    merged_local = normed.reshape(patch_rows // 4, 4 * VIT_D)
    token_rows = lax.all_gather(merged_local, "tp", axis=0, tiled=True)
    embedded_sum = jnp.dot(
        token_rows,
        lax.all_gather(merger_weight, ("img", "seq"), axis=0, tiled=True),
        preferred_element_type=jnp.float32,
    )
    embedded = lax.optimization_barrier(embedded_sum.astype(jnp.bfloat16))
    embedded_wide = embedded.astype(jnp.float32)
    square_sums = lax.psum(jnp.sum(embedded_wide * embedded_wide, axis=-1), "tp")
    lm_normed = (embedded_wide * lax.rsqrt(square_sums[:, None] / D + 1e-06) * lm_norm_gain).astype(
        jnp.bfloat16
    )
    kv_terms = jnp.dot(
        lm_normed,
        lax.all_gather(kv_weight, ("img", "seq"), axis=1, tiled=True),
        preferred_element_type=jnp.float32,
    )
    visual_count = kv_terms.shape[0]
    kv_terms = kv_terms.reshape(visual_count, 2, KVH, HD)
    visual_kv = lax.psum_scatter(
        kv_terms.astype(jnp.bfloat16), "tp", scatter_dimension=2, tiled=True
    )
    span_rows = queries.shape[1]
    kv_local = span_kv.shape[3]
    groups = HQ // KVH
    lm_scaling = HD ** (-0.5)
    grouped = queries[0].reshape(span_rows, kv_local, groups, HD)
    causal = jnp.arange(span_rows)[:, None] >= jnp.arange(span_rows)[None, :]
    near_scores = (
        jnp.einsum("ckgd,nkd->kgcn", grouped, span_kv[0, :, 0], preferred_element_type=jnp.float32)
        * lm_scaling
    )
    initial = (
        jnp.full((kv_local, groups, span_rows), masked_score, jnp.float32),
        jnp.zeros((kv_local, groups, span_rows), jnp.float32),
        jnp.zeros((kv_local, groups, span_rows, HD), jnp.float32),
    )
    initial = fold_block(
        initial, near_scores, causal[None, None], span_kv[0, :, 1], "kgcn,nkd->kgcd"
    )
    visual_total = patch_total // 4
    key_piece = lax.all_gather(visual_kv[:, 0], "seq", axis=0, tiled=True)
    value_piece = lax.all_gather(visual_kv[:, 1], "seq", axis=0, tiled=True)
    blocks = key_piece.shape[0] // visual_count
    key_blocks = key_piece.reshape(blocks, visual_count, kv_local, HD)
    value_blocks = value_piece.reshape(blocks, visual_count, kv_local, HD)
    offsets = jnp.arange(blocks, dtype=jnp.int32) * visual_count

    def visual_advance(state, inputs):
        key_block, value_block, offset = inputs
        usable = offset + jnp.arange(visual_count, dtype=jnp.int32) < visual_total
        scores = (
            jnp.einsum("ckgd,nkd->kgcn", grouped, key_block, preferred_element_type=jnp.float32)
            * lm_scaling
        )
        return (
            fold_block(state, scores, usable[None, None, None, :], value_block, "kgcn,nkd->kgcd"),
            None,
        )

    result, _ = lax.scan(visual_advance, initial, (key_blocks, value_blocks, offsets))
    peak, weight_sum, blended = result
    result = jnp.transpose(blended / weight_sum[..., None], (2, 0, 1, 3))
    return result.reshape(span_rows, kv_local * groups, HD).astype(jnp.bfloat16)[None]


def swap_pairs(plane, seqs, tps, move):
    pairs = []
    for x in range(plane):
        for c in range(2):
            for s in range(seqs):
                for t in range(tps):
                    x2, c2, s2 = move(x, c, s)
                    pairs.append((((x * 2 + c) * seqs + s) * tps + t, ((x2 * 2 + c2) * seqs + s2) * tps + t))
    return pairs


def fast_local(
    vit_qkv,
    patch_counts,
    vit_out_weight,
    vit_norm_gain,
    merger_weight,
    lm_norm_gain,
    kv_weight,
    queries,
    span_kv,
):
    everything = ("x", "c", "seq", "tp")
    plane = lax.axis_size("x")
    seqs = lax.axis_size("seq")
    tps = lax.axis_size("tp")
    x, c, s, t = (lax.axis_index(name) for name in everything)
    owners = seqs * tps
    patch_rows = vit_qkv.shape[1]
    token_rows = patch_rows // 4
    patch_total = patch_counts[0]
    share = VIT_D // owners
    heads = VIT_HEADS // owners

    def swap(value, move):
        return lax.ppermute(value, everything, swap_pairs(plane, seqs, tps, move))

    def other_core(x, c, s):
        return x, 1 - c, s

    def first_hop(x, c, s):
        return (1 - x, c, s) if c == 0 else (x, c, 1 - s)

    def second_hop(x, c, s):
        return (x, c, 1 - s) if c == 0 else (1 - x, c, s)

    other_rows = swap(merger_weight, other_core)
    kv_one = kv_weight[None]
    kv_hop = swap(kv_one, first_hop)
    kv_two = jnp.concatenate([kv_one, kv_hop])
    kv_far = swap(kv_two, second_hop)
    kv_four = jnp.concatenate([kv_two, kv_far])
    kv_other = swap(kv_four, other_core)

    packed = vit_qkv[0].reshape(patch_rows, 3, owners, share)
    packed = jnp.transpose(packed, (2, 0, 1, 3)).reshape(owners, patch_rows, 3 * share)
    spread = lax.all_to_all(packed, ("seq", "tp"), split_axis=0, concat_axis=0, tiled=True)
    patches = owners * patch_rows
    spread = spread.reshape(patches, 3, heads, VIT_HDIM)
    scores = jnp.einsum(
        "qhd,khd->hqk", spread[:, 0], spread[:, 1], preferred_element_type=jnp.float32
    ) * VIT_HDIM ** (-0.5)
    usable = jnp.arange(patches, dtype=jnp.int32) < patch_total
    scores = jnp.where(usable, scores, masked_score)
    weights = jnp.exp(scores - jnp.max(scores, axis=-1, keepdims=True))
    weight_sum = jnp.sum(weights, axis=-1)
    blended = jnp.einsum(
        "hqk,khd->qhd", weights.astype(jnp.bfloat16), spread[:, 2], preferred_element_type=jnp.float32
    )
    blended = blended / weight_sum.T[..., None]
    attended = blended.astype(jnp.bfloat16).reshape(owners, patch_rows, share)
    attended = lax.all_to_all(attended, ("seq", "tp"), split_axis=0, concat_axis=0, tiled=True)
    attended = jnp.transpose(attended, (1, 0, 2)).reshape(patch_rows, VIT_D)

    hidden = jnp.dot(attended, vit_out_weight, preferred_element_type=jnp.float32)
    patch_ids = (s * tps + t) * patch_rows + jnp.arange(patch_rows, dtype=jnp.int32)
    hidden = jnp.where((patch_ids < patch_total)[:, None], hidden, 0.0)
    centred = hidden - jnp.mean(hidden, axis=-1, keepdims=True)
    spread_sq = jnp.mean(centred * centred, axis=-1, keepdims=True)
    normed = (centred * lax.rsqrt(spread_sq + 1e-06) * vit_norm_gain).astype(jnp.bfloat16)

    rows_local = merger_weight.shape[0]
    merged = normed.reshape(token_rows, plane, 2, seqs, rows_local)
    merged = jnp.where(c == 0, merged, merged[:, :, ::-1])
    merged = jnp.transpose(merged, (1, 3, 0, 2, 4)).reshape(plane, seqs, 1, token_rows, 2 * rows_local)
    merged = jnp.broadcast_to(merged, (plane, seqs, tps, token_rows, 2 * rows_local))
    merged = merged.reshape(plane * owners, token_rows, 2 * rows_local)
    tokens = lax.all_to_all(merged, ("x", "seq", "tp"), split_axis=0, concat_axis=0, tiled=True)
    half = tps * token_rows
    tokens = tokens.reshape(plane * seqs, half, 2 * rows_local)

    def quarter(xq, sq):
        return xq * seqs + sq

    far = quarter(1 - x, 1 - s)
    order = jnp.where(
        c == 0,
        jnp.stack([far, quarter(1 - x, s), quarter(x, 1 - s), quarter(x, s)]),
        jnp.stack([far, quarter(x, 1 - s), quarter(1 - x, s), quarter(x, s)]),
    )
    tokens = jnp.concatenate(
        [lax.dynamic_slice_in_dim(tokens, order[k], 1, 0) for k in range(4)]
    ).reshape(4 * half, 2 * rows_local)
    partial = jnp.dot(tokens[:, :rows_local], merger_weight, preferred_element_type=jnp.float32)
    partial = partial + jnp.dot(
        tokens[:, rows_local:], other_rows, preferred_element_type=jnp.float32
    )
    sent = partial[: 2 * half].astype(jnp.bfloat16)
    kept = partial[2 * half :] + swap(sent, first_hop).astype(jnp.float32)
    sent = kept[:half].astype(jnp.bfloat16)
    embedded = kept[half:] + swap(sent, second_hop).astype(jnp.float32)

    squares = jnp.sum(embedded * embedded, axis=-1)
    gained = (embedded * lm_norm_gain).astype(jnp.bfloat16)

    def project(block):
        return jnp.dot(gained, block, preferred_element_type=jnp.float32).astype(jnp.bfloat16)

    columns = []
    for core_step in range(2):
        for far_step in range(2):
            for hop_step in range(2):
                bank = kv_other if core_step else kv_four
                columns.append(project(bank[far_step * 2 + hop_step]))
    stacked = jnp.stack(columns)
    slots = []
    for kind in range(2):
        for dest in range(tps):
            block_c, block_s = dest // seqs, dest % seqs
            dx = x ^ kind
            ds = s ^ block_s
            dc = c ^ block_c
            owner_core = block_c
            hop = jnp.where(owner_core == 0, dx, ds)
            fars = jnp.where(owner_core == 0, ds, dx)
            slots.append((dc * 2 + fars) * 2 + hop)
    placed = jnp.stack([lax.dynamic_index_in_dim(stacked, k, 0, False) for k in slots])
    placed = placed.reshape(2, tps, half, -1)
    payload = jnp.concatenate([placed[0], placed[1]], axis=-1)
    coarse = squares.astype(jnp.bfloat16)
    fine = (squares - coarse.astype(jnp.float32)).astype(jnp.bfloat16)
    lane = jnp.arange(128, dtype=jnp.int32)
    extra = jnp.where(lane == 0, coarse[:, None], jnp.where(lane == 1, fine[:, None], 0))
    extra = jnp.broadcast_to(extra.astype(jnp.bfloat16)[None], (tps, half, 128))
    payload = jnp.concatenate([payload, extra], axis=-1)
    sums = lax.all_to_all(payload, "tp", split_axis=0, concat_axis=0, tiled=True)
    sums = jnp.sum(sums.astype(jnp.float32), axis=0)
    width = placed.shape[-1]
    total = sums[:, 2 * width] + sums[:, 2 * width + 1]
    visual = sums[:, : 2 * width] * lax.rsqrt(total / D + 1e-06)[:, None]
    visual = visual.astype(jnp.bfloat16)
    twin = swap(visual, lambda x, c, s: (x, c, 1 - s))
    first = jnp.where(s == 0, visual, twin)
    second = jnp.where(s == 0, twin, visual)
    visual = jnp.concatenate([first, second]).reshape(2 * half, 2, -1, HD)

    span_rows = queries.shape[1]
    kv_local = span_kv.shape[3]
    groups = HQ // KVH
    lm_scaling = HD ** (-0.5)
    grouped = queries[0].reshape(span_rows, kv_local, groups, HD)
    causal = jnp.arange(span_rows)[:, None] >= jnp.arange(span_rows)[None, :]
    near_scores = (
        jnp.einsum("ckgd,nkd->kgcn", grouped, span_kv[0, :, 0], preferred_element_type=jnp.float32)
        * lm_scaling
    )
    initial = (
        jnp.full((kv_local, groups, span_rows), masked_score, jnp.float32),
        jnp.zeros((kv_local, groups, span_rows), jnp.float32),
        jnp.zeros((kv_local, groups, span_rows, HD), jnp.float32),
    )
    state = fold_block(
        initial, near_scores, causal[None, None], span_kv[0, :, 1], "kgcn,nkd->kgcd"
    )
    seen = jnp.arange(2 * half, dtype=jnp.int32) < patch_total // 4
    far_scores = (
        jnp.einsum("ckgd,nkd->kgcn", grouped, visual[:, 0], preferred_element_type=jnp.float32)
        * lm_scaling
    )
    state = fold_block(state, far_scores, seen[None, None, None], visual[:, 1], "kgcn,nkd->kgcd")
    peak, weight_sum, blended = state
    result = jnp.transpose(blended / weight_sum[..., None], (2, 0, 1, 3))
    return result.reshape(span_rows, kv_local * groups, HD).astype(jnp.bfloat16)[None]


def solution(mesh):
    sizes = dict(mesh.shape)
    images, seqs, tps = (sizes[name] for name in ("img", "seq", "tp"))
    suited = (
        images == 4
        and seqs == 2
        and images * seqs == 2 * tps
        and VIT_HEADS % (seqs * tps) == 0
        and KVH % tps == 0
    )
    if not suited:
        placed = (
            P("img", ("seq", "tp"), None, None),
            P("img"),
            P(),
            P(),
            P(("img", "seq"), "tp"),
            P("tp"),
            P("tp", ("img", "seq")),
            P("img", "seq", "tp", None),
            P("img", "seq", None, "tp", None),
        )
        return jax.shard_map(
            local, mesh=mesh, in_specs=placed, out_specs=P("img", "seq", "tp", None), check_vma=False
        )
    split = Mesh(
        mesh.devices.reshape(images // 2, 2, seqs, tps), ("x", "c", "seq", "tp")
    )
    image = ("x", "c")
    placed = (
        P(image, ("seq", "tp"), None, None),
        P(image),
        P(),
        P(),
        P(("x", "c", "seq"), "tp"),
        P("tp"),
        P("tp", ("x", "c", "seq")),
        P(image, "seq", "tp", None),
        P(image, "seq", None, "tp", None),
    )
    return jax.shard_map(
        fast_local, mesh=split, in_specs=placed, out_specs=P(image, "seq", "tp", None), check_vma=False
    )
```

```python
import math

import jax
import jax.numpy as jnp
from jax import lax
from jax.experimental import pallas as pl
from jax.experimental.pallas import tpu as pltpu
from jax.sharding import Mesh
from jax.sharding import PartitionSpec as P

VIT_D = 1280
VIT_HEADS = 16
VIT_HDIM = 80
D = 8192
HQ = 64
KVH = 8
HD = 128


masked_score = -1e30
LOG2E = math.log2(math.e)


def fold_block(running, scores, usable, value_block, forms):
    peak, weight_sum, blended = running
    scores = jnp.where(usable, scores, masked_score)
    new_peak = jnp.maximum(peak, jnp.max(scores, axis=-1))
    weights = jnp.where(usable, jnp.exp(scores - new_peak[..., None]), 0.0)
    decay = jnp.exp(peak - new_peak)
    weight_sum = weight_sum * decay + jnp.sum(weights, axis=-1)
    blended = blended * decay[..., None] + jnp.einsum(
        forms, weights.astype(jnp.bfloat16), value_block, preferred_element_type=jnp.float32
    )
    return (new_peak, weight_sum, blended)


def local(
    vit_qkv,
    patch_counts,
    vit_out_weight,
    vit_norm_gain,
    merger_weight,
    lm_norm_gain,
    kv_weight,
    queries,
    span_kv,
):
    patch_rows = vit_qkv.shape[1]
    tp_count = lax.axis_size("tp")
    seq_index = lax.axis_index("seq")
    tp_index = lax.axis_index("tp")
    patch_total = patch_counts[0]
    local_qkv = vit_qkv[0].reshape(patch_rows, 3, VIT_HEADS, VIT_HDIM)
    scaling = VIT_HDIM ** (-0.5)
    spread = lax.all_to_all(local_qkv, "seq", split_axis=2, concat_axis=0, tiled=True)
    local_rows = spread.shape[0]

    def seq_rows(index):
        source = index // local_rows
        within = index % local_rows
        return (within // patch_rows * tp_count + source) * patch_rows + within % patch_rows

    heads_local = spread.shape[2]
    query_count = spread.shape[0]
    query_rows = spread[:, 0]
    running = (
        jnp.full((heads_local, query_count), masked_score, jnp.float32),
        jnp.zeros((heads_local, query_count), jnp.float32),
        jnp.zeros((heads_local, query_count, VIT_HDIM), jnp.float32),
    )
    make_heads_local = query_rows.shape[1]
    key_piece = lax.all_gather(spread[:, 1], "tp", axis=0, tiled=True)
    value_piece = lax.all_gather(spread[:, 2], "tp", axis=0, tiled=True)
    blocks = key_piece.shape[0] // local_rows
    key_blocks = key_piece.reshape(blocks, local_rows, make_heads_local, VIT_HDIM)
    value_blocks = value_piece.reshape(blocks, local_rows, make_heads_local, VIT_HDIM)
    offsets = jnp.arange(blocks, dtype=jnp.int32) * local_rows

    def make_advance(state, inputs):
        key_block, value_block, offset = inputs
        usable = seq_rows(offset + jnp.arange(local_rows, dtype=jnp.int32)) < patch_total
        scores = (
            jnp.einsum("qhd,khd->hqk", query_rows, key_block, preferred_element_type=jnp.float32)
            * scaling
        )
        return (fold_block(state, scores, usable[None, None, :], value_block, "hqk,khd->hqd"), None)

    result, _ = lax.scan(make_advance, running, (key_blocks, value_blocks, offsets))
    state = result
    peak, weight_sum, blended = state
    returned = lax.all_to_all(
        jnp.transpose(blended / weight_sum[..., None], (1, 0, 2)).astype(jnp.bfloat16),
        "seq",
        split_axis=0,
        concat_axis=1,
        tiled=True,
    )
    attended = returned.reshape(patch_rows, VIT_D)
    hidden = jnp.dot(attended, vit_out_weight, preferred_element_type=jnp.float32)
    patch_ids = (seq_index * tp_count + tp_index) * patch_rows + jnp.arange(
        patch_rows, dtype=jnp.int32
    )
    hidden = jnp.where((patch_ids < patch_total)[:, None], hidden, 0.0)
    centred = hidden - jnp.mean(hidden, axis=-1, keepdims=True)
    spread_sq = jnp.mean(centred * centred, axis=-1, keepdims=True)
    normed = (centred * lax.rsqrt(spread_sq + 1e-06) * vit_norm_gain).astype(jnp.bfloat16)
    merged_local = normed.reshape(patch_rows // 4, 4 * VIT_D)
    token_rows = lax.all_gather(merged_local, "tp", axis=0, tiled=True)
    embedded_sum = jnp.dot(
        token_rows,
        lax.all_gather(merger_weight, ("img", "seq"), axis=0, tiled=True),
        preferred_element_type=jnp.float32,
    )
    embedded = lax.optimization_barrier(embedded_sum.astype(jnp.bfloat16))
    embedded_wide = embedded.astype(jnp.float32)
    square_sums = lax.psum(jnp.sum(embedded_wide * embedded_wide, axis=-1), "tp")
    lm_normed = (embedded_wide * lax.rsqrt(square_sums[:, None] / D + 1e-06) * lm_norm_gain).astype(
        jnp.bfloat16
    )
    kv_terms = jnp.dot(
        lm_normed,
        lax.all_gather(kv_weight, ("img", "seq"), axis=1, tiled=True),
        preferred_element_type=jnp.float32,
    )
    visual_count = kv_terms.shape[0]
    kv_terms = kv_terms.reshape(visual_count, 2, KVH, HD)
    visual_kv = lax.psum_scatter(
        kv_terms.astype(jnp.bfloat16), "tp", scatter_dimension=2, tiled=True
    )
    span_rows = queries.shape[1]
    kv_local = span_kv.shape[3]
    groups = HQ // KVH
    lm_scaling = HD ** (-0.5)
    grouped = queries[0].reshape(span_rows, kv_local, groups, HD)
    causal = jnp.arange(span_rows)[:, None] >= jnp.arange(span_rows)[None, :]
    near_scores = (
        jnp.einsum("ckgd,nkd->kgcn", grouped, span_kv[0, :, 0], preferred_element_type=jnp.float32)
        * lm_scaling
    )
    initial = (
        jnp.full((kv_local, groups, span_rows), masked_score, jnp.float32),
        jnp.zeros((kv_local, groups, span_rows), jnp.float32),
        jnp.zeros((kv_local, groups, span_rows, HD), jnp.float32),
    )
    initial = fold_block(
        initial, near_scores, causal[None, None], span_kv[0, :, 1], "kgcn,nkd->kgcd"
    )
    visual_total = patch_total // 4
    key_piece = lax.all_gather(visual_kv[:, 0], "seq", axis=0, tiled=True)
    value_piece = lax.all_gather(visual_kv[:, 1], "seq", axis=0, tiled=True)
    blocks = key_piece.shape[0] // visual_count
    key_blocks = key_piece.reshape(blocks, visual_count, kv_local, HD)
    value_blocks = value_piece.reshape(blocks, visual_count, kv_local, HD)
    offsets = jnp.arange(blocks, dtype=jnp.int32) * visual_count

    def visual_advance(state, inputs):
        key_block, value_block, offset = inputs
        usable = offset + jnp.arange(visual_count, dtype=jnp.int32) < visual_total
        scores = (
            jnp.einsum("ckgd,nkd->kgcn", grouped, key_block, preferred_element_type=jnp.float32)
            * lm_scaling
        )
        return (
            fold_block(state, scores, usable[None, None, None, :], value_block, "kgcn,nkd->kgcd"),
            None,
        )

    result, _ = lax.scan(visual_advance, initial, (key_blocks, value_blocks, offsets))
    peak, weight_sum, blended = result
    result = jnp.transpose(blended / weight_sum[..., None], (2, 0, 1, 3))
    return result.reshape(span_rows, kv_local * groups, HD).astype(jnp.bfloat16)[None]


def whole(*arrays):
    return [pl.BlockSpec(memory_space=pltpu.SMEM if a.dtype == jnp.int32 else pltpu.VMEM) for a in arrays]


def call(body, outs, *arrays, scratch=(), cost=None):
    many = isinstance(outs, (tuple, list))
    return pl.pallas_call(
        body,
        out_shape=outs,
        in_specs=whole(*arrays),
        out_specs=jax.tree.map(lambda _: pl.BlockSpec(memory_space=pltpu.VMEM), outs),
        scratch_shapes=list(scratch),
        cost_estimate=cost,
    )(*arrays)


def pack_heads(rows, owners):
    patches, kinds, width = rows.shape
    share = width // owners

    def body(rows_ref, out_ref):
        for kind in range(kinds):
            values = rows_ref[:, kind, :]
            for owner in range(owners):
                out_ref[owner, :, kind * share : (kind + 1) * share] = values[
                    :, owner * share : (owner + 1) * share
                ]

    return call(body, jax.ShapeDtypeStruct((owners, patches, kinds * share), rows.dtype), rows)


def vision_attention(spread, patch_counts):
    owners, patches, width = spread.shape
    share = width // 3
    heads = share // VIT_HDIM
    slots = owners * patches
    block = 128
    lanes = 128
    tail = share - lanes
    folds = lanes // tail
    tail_rows = patches // folds
    factor = VIT_HDIM ** (-0.5) * LOG2E

    def body(count_ref, spread_ref, out_ref):
        values = spread_ref[...].reshape(slots, width)
        keys = values[:, share : 2 * share]
        last = values[:, 2 * share :]
        usable = lax.broadcasted_iota(jnp.int32, (1, slots), 1) < count_ref[0]
        lane_head = lax.broadcasted_iota(jnp.int32, (1, share), 1) // VIT_HDIM
        for start in range(0, slots, block):
            query = values[start : start + block, :share]
            result = jnp.zeros((block, share), jnp.float32)
            for head in range(heads):
                own = lane_head == head
                picked = jnp.where(own, query, jnp.zeros_like(query))
                scores = lax.dot_general(
                    picked, keys, (((1,), (1,)), ((), ())), preferred_element_type=jnp.float32
                )
                scores = jnp.where(usable, scores, masked_score)
                peak = jnp.max(scores, axis=-1, keepdims=True)
                weights = jnp.exp2((scores - peak) * factor)
                weight_sum = jnp.sum(weights, axis=-1, keepdims=True)
                blended = jnp.dot(
                    weights.astype(jnp.bfloat16), last, preferred_element_type=jnp.float32
                )
                result = jnp.where(own, blended / weight_sum, result)
            for part in range(block // patches):
                piece = result[part * patches : (part + 1) * patches]
                owner = start // patches + part
                out_ref[owner, :patches, :] = piece[:, :lanes].astype(jnp.bfloat16)
                out_ref[owner, patches:, :] = jnp.concatenate(
                    [piece[k * tail_rows : (k + 1) * tail_rows, lanes:] for k in range(folds)], axis=1
                ).astype(jnp.bfloat16)

    out = jax.ShapeDtypeStruct((owners, patches + tail_rows, lanes), jnp.bfloat16)
    return call(body, out, patch_counts, spread)


def project_norm(places, returned, out_weight, gain, plane, seqs, tps, rows_local):
    owners, packed_rows, lanes = returned.shape
    width = out_weight.shape[0]
    share = width // owners
    tail = share - lanes
    folds = lanes // tail
    patches = packed_rows * folds // (folds + 1)
    tail_rows = packed_rows - patches
    token_rows = patches // 4
    tiles = width // lanes

    def body(places_ref, returned_ref, weight_ref, gain_ref, out_ref, rows_ref):
        pieces = []
        for owner in range(owners):
            pieces.append(returned_ref[owner, :patches, :].astype(jnp.float32))
            rest = returned_ref[owner, patches:, :].astype(jnp.float32)
            pieces.append(
                jnp.concatenate([rest[:, k * tail : (k + 1) * tail] for k in range(folds)], axis=0)
            )
        attended = jnp.concatenate(pieces, axis=1).astype(jnp.bfloat16)
        hidden = jnp.dot(attended, weight_ref[...], preferred_element_type=jnp.float32)
        ids = lax.broadcasted_iota(jnp.int32, (patches, 1), 0) + places_ref[1]
        hidden = jnp.where(ids < places_ref[0], hidden, 0.0)
        centred = hidden - jnp.mean(hidden, axis=-1, keepdims=True)
        spread_sq = jnp.mean(centred * centred, axis=-1, keepdims=True)
        normed = centred * lax.rsqrt(spread_sq + 1e-06) * gain_ref[...]
        for tile in range(tiles):
            rows_ref[tile] = normed[:, tile * lanes : (tile + 1) * lanes]
        even = places_ref[2] == 0
        for xq in range(plane):
            pair = [
                jnp.concatenate(
                    [
                        rows_ref[tile, pl.ds(2 * xq + core, token_rows, stride=4), :]
                        for tile in range(tiles)
                    ],
                    axis=1,
                ).astype(jnp.bfloat16)
                for core in range(2)
            ]
            first = jnp.where(even, pair[0], pair[1])
            second = jnp.where(even, pair[1], pair[0])
            for sq in range(seqs):
                for tq in range(tps):
                    place = (xq * seqs + sq) * tps + tq
                    cut = slice(sq * rows_local, (sq + 1) * rows_local)
                    out_ref[place, :, :rows_local] = first[:, cut]
                    out_ref[place, :, rows_local:] = second[:, cut]

    out = jax.ShapeDtypeStruct((plane * seqs * tps, token_rows, 2 * rows_local), jnp.bfloat16)
    return call(
        body, out, places, returned, out_weight, gain[None],
        scratch=[pltpu.VMEM((tiles, patches, lanes), jnp.float32)],
    )


def merge_partial(order, tokens, own_weight, other_weight):
    quarters, half, depth = tokens.shape
    rows_local, columns = own_weight.shape
    block = 512

    def body(order_ref, tokens_ref, own_ref, other_ref, sent_ref, kept_ref):
        rows = jnp.concatenate([tokens_ref[order_ref[k]] for k in range(quarters)], axis=0)
        result = jnp.dot(rows[:, :rows_local], own_ref[...], preferred_element_type=jnp.float32)
        result = result + jnp.dot(
            rows[:, rows_local:], other_ref[...], preferred_element_type=jnp.float32
        )
        sent_ref[...] = result[: 2 * half].astype(jnp.bfloat16)
        kept_ref[...] = result[2 * half :]

    weight_spec = pl.BlockSpec((rows_local, block), lambda n: (0, n))
    out_spec = pl.BlockSpec((2 * half, block), lambda n: (0, n))
    return pl.pallas_call(
        body,
        grid=(columns // block,),
        out_shape=(
            jax.ShapeDtypeStruct((2 * half, columns), jnp.bfloat16),
            jax.ShapeDtypeStruct((2 * half, columns), jnp.float32),
        ),
        in_specs=[
            pl.BlockSpec(memory_space=pltpu.SMEM),
            pl.BlockSpec((quarters, half, depth), lambda n: (0, 0, 0)),
            weight_spec,
            weight_spec,
        ],
        out_specs=(out_spec, out_spec),
    )(order, tokens, own_weight, other_weight)


def project_visual(places, kept, received, gain, blocks, tps):
    half, depth = kept.shape
    width = blocks[0].shape[1]
    count = len(blocks)
    extra = 16

    def body(places_ref, kept_ref, received_ref, gain_ref, *refs):
        block_refs, out_ref = refs[:count], refs[count]
        buffers, sems = refs[count + 1 :]
        copies = [
            pltpu.make_async_copy(block_refs[k], buffers.at[k], sems.at[k]) for k in range(count)
        ]
        for copy in copies:
            copy.start()
        embedded = kept_ref[...] + received_ref[...].astype(jnp.float32)
        squares = jnp.sum(embedded * embedded, axis=-1, keepdims=True)
        gained = (embedded * gain_ref[...]).astype(jnp.bfloat16)
        flat = jnp.broadcast_to(squares, (half, 128)).T[:extra]
        coarse = flat.astype(jnp.bfloat16).astype(jnp.float32)
        upper = lax.broadcasted_iota(jnp.int32, (extra, half), 0) < extra // 2
        both = jnp.where(upper, coarse, flat - coarse)
        both = jnp.concatenate([both, jnp.zeros((extra, width - half), jnp.float32)], axis=1)
        both = both.astype(jnp.bfloat16)
        for dest in range(tps):
            out_ref[dest, 2 * half :, :] = both
        for k in range(count):
            copies[k].wait()
            term = jnp.dot(gained, buffers[k], preferred_element_type=jnp.float32)
            row = pl.multiple_of(places_ref[2 * k + 1] * half, half)
            out_ref[places_ref[2 * k], pl.ds(row, half), :] = term.astype(jnp.bfloat16)

    out = jax.ShapeDtypeStruct((tps, 2 * half + extra, width), jnp.bfloat16)
    return pl.pallas_call(
        body,
        out_shape=out,
        in_specs=[pl.BlockSpec(memory_space=pltpu.SMEM)]
        + [pl.BlockSpec(memory_space=pltpu.VMEM)] * 3
        + [pl.BlockSpec(memory_space=pl.ANY)] * count,
        out_specs=pl.BlockSpec(memory_space=pltpu.VMEM),
        scratch_shapes=[
            pltpu.VMEM((count, depth, width), jnp.bfloat16),
            pltpu.SemaphoreType.DMA((count,)),
        ],
    )(places, kept, received, gain[None], *blocks)


def finish_visual(sums, half):
    width = sums.shape[2]

    def body(sums_ref, out_ref):
        total = jnp.sum(sums_ref[...].astype(jnp.float32), axis=0)
        flat = total[2 * half : 2 * half + 8] + total[2 * half + 8 :]
        squares = jnp.broadcast_to(flat[:1, :128], (128, 128)).T[:half, :1]
        scale = lax.rsqrt(squares / D + 1e-06)
        out_ref[:half] = (total[:half] * scale).astype(jnp.bfloat16)
        out_ref[half:] = (total[half : 2 * half] * scale).astype(jnp.bfloat16)

    return call(body, jax.ShapeDtypeStruct((2 * half, width), jnp.bfloat16), sums)


def split_queries(block, kv_local):
    tokens, heads, width = block.shape
    groups = heads // kv_local
    wide = block.astype(jnp.float32).reshape(tokens, kv_local, groups, width)
    return [
        wide[:, k].reshape(tokens * groups, width).astype(jnp.bfloat16) for k in range(kv_local)
    ]


def prompt_own(queries, span_kv, kv_head):
    tokens, heads, width = queries.shape
    kv_local = span_kv.shape[2]
    groups = heads // kv_local
    block = 128
    rows = block * groups
    factor = HD ** (-0.5) * LOG2E

    def body(queries_ref, span_ref, out_ref, stats_ref):
        for index in range(tokens // block):
            start = index * block
            query = split_queries(queries_ref[start : start + block], kv_local)[kv_head]
            extent = start + block
            keys = span_ref[:extent, 0, kv_head, :]
            values = span_ref[:extent, 1, kv_head, :]
            scores = lax.dot_general(
                keys, query, (((1,), (1,)), ((), ())), preferred_element_type=jnp.float32
            )
            key_ids = lax.broadcasted_iota(jnp.int32, (extent, rows), 0)
            token_ids = start + lax.broadcasted_iota(jnp.int32, (extent, rows), 1) // groups
            scores = jnp.where(key_ids <= token_ids, scores, masked_score)
            peak = jnp.max(scores, axis=0, keepdims=True)
            weights = jnp.exp2((scores - peak) * factor)
            cut = slice(start * groups, extent * groups)
            stats_ref[0:1, cut] = peak
            stats_ref[1:2, cut] = jnp.sum(weights, axis=0, keepdims=True)
            out_ref[:, cut] = lax.dot_general(
                values, weights.astype(jnp.bfloat16), (((0,), (0,)), ((), ())),
                preferred_element_type=jnp.float32,
            )

    outs = (
        jax.ShapeDtypeStruct((width, tokens * groups), jnp.float32),
        jax.ShapeDtypeStruct((2, tokens * groups), jnp.float32),
    )
    return call(body, outs, queries, span_kv)


def prompt_visual(places, queries, own, twin, near, half):
    tokens, heads, width = queries.shape
    kv_local = len(near)
    groups = heads // kv_local
    block = 128
    rows = block * groups
    factor = HD ** (-0.5) * LOG2E

    def body(places_ref, queries_ref, own_ref, twin_ref, *refs):
        near_refs, out_ref = refs[:-1], refs[-1]
        split = split_queries(queries_ref[...], kv_local)
        ids = lax.broadcasted_iota(jnp.int32, (2 * half, 1), 0)
        ids = jnp.where(ids < half, ids + places_ref[1], ids - half + places_ref[2])
        seen = ids < places_ref[0]
        results = []
        for k in range(kv_local):
            cut = slice(k * width, (k + 1) * width)
            keys = jnp.concatenate([own_ref[:half, cut], twin_ref[:half, cut]], axis=0)
            values = jnp.concatenate([own_ref[half:, cut], twin_ref[half:, cut]], axis=0)
            scores = lax.dot_general(
                keys, split[k], (((1,), (1,)), ((), ())), preferred_element_type=jnp.float32
            )
            scores = jnp.where(seen, scores, masked_score)
            stats = near_refs[2 * k + 1][...]
            peak = jnp.maximum(stats[0:1], jnp.max(scores, axis=0, keepdims=True))
            weights = jnp.exp2((scores - peak) * factor)
            decay = jnp.exp2((stats[0:1] - peak) * factor)
            total = stats[1:2] * decay + jnp.sum(weights, axis=0, keepdims=True)
            blended = lax.dot_general(
                values, weights.astype(jnp.bfloat16), (((0,), (0,)), ((), ())),
                preferred_element_type=jnp.float32,
            )
            blended = (blended + near_refs[2 * k][...] * decay) / total
            results.append(blended.T.reshape(block, 1, groups, width))
        joined = jnp.concatenate(results, axis=1).reshape(block, heads, width)
        out_ref[...] = joined.astype(jnp.bfloat16)

    query_spec = pl.BlockSpec((block, heads, width), lambda n: (n, 0, 0))
    fixed = pl.BlockSpec((2 * half, kv_local * width), lambda n: (0, 0))
    near_specs = [
        pl.BlockSpec((width, rows), lambda n: (0, n)),
        pl.BlockSpec((2, rows), lambda n: (0, n)),
    ] * kv_local
    return pl.pallas_call(
        body,
        grid=(tokens // block,),
        out_shape=jax.ShapeDtypeStruct(queries.shape, jnp.bfloat16),
        in_specs=[pl.BlockSpec(memory_space=pltpu.SMEM), query_spec, fixed, fixed] + near_specs,
        out_specs=query_spec,
    )(places, queries, own, twin, *[part for pair in near for part in pair])


def swap_pairs(plane, seqs, tps, move):
    pairs = []
    for x in range(plane):
        for c in range(2):
            for s in range(seqs):
                for t in range(tps):
                    x2, c2, s2 = move(x, c, s)
                    pairs.append((((x * 2 + c) * seqs + s) * tps + t, ((x2 * 2 + c2) * seqs + s2) * tps + t))
    return pairs


def fast_local(
    vit_qkv,
    patch_counts,
    vit_out_weight,
    vit_norm_gain,
    merger_weight,
    lm_norm_gain,
    kv_weight,
    queries,
    span_kv,
):
    everything = ("x", "c", "seq", "tp")
    plane = lax.axis_size("x")
    seqs = lax.axis_size("seq")
    tps = lax.axis_size("tp")
    x, c, s, t = (lax.axis_index(name) for name in everything)
    owners = seqs * tps
    patch_rows = vit_qkv.shape[1]
    token_rows = patch_rows // 4
    half = tps * token_rows
    rows_local = merger_weight.shape[0]
    patch_total = patch_counts[0]

    def swap(value, move):
        return lax.ppermute(value, everything, swap_pairs(plane, seqs, tps, move))

    def exchange(value, names):
        return lax.all_to_all(value, names, split_axis=0, concat_axis=0, tiled=True)

    def other_core(x, c, s):
        return x, 1 - c, s

    def first_hop(x, c, s):
        return (1 - x, c, s) if c == 0 else (x, c, 1 - s)

    def second_hop(x, c, s):
        return (x, c, 1 - s) if c == 0 else (1 - x, c, s)

    def other_seq(x, c, s):
        return x, c, 1 - s

    spread = exchange(pack_heads(vit_qkv[0], owners), ("seq", "tp"))
    other_rows = swap(merger_weight, other_core)

    near_block = swap(kv_weight, first_hop)
    side_block = swap(kv_weight, second_hop)
    far_block = swap(near_block, second_hop)
    chip_blocks = [kv_weight, near_block, side_block, far_block]
    kv_blocks = chip_blocks + [swap(block, other_core) for block in chip_blocks]

    near = [prompt_own(queries[0], span_kv[0], k) for k in range(span_kv.shape[3])]

    returned = exchange(vision_attention(spread, patch_counts), ("seq", "tp"))
    places = jnp.stack([patch_total, (s * tps + t) * patch_rows, c]).astype(jnp.int32)
    merged = project_norm(
        places, returned, vit_out_weight, vit_norm_gain, plane, seqs, tps, rows_local
    )

    tokens = exchange(merged, ("x", "seq", "tp")).reshape(plane * seqs, half, 2 * rows_local)

    def quarter(xq, sq):
        return xq * seqs + sq

    between = jnp.where(
        c == 0,
        jnp.stack([quarter(1 - x, s), quarter(x, 1 - s)]),
        jnp.stack([quarter(x, 1 - s), quarter(1 - x, s)]),
    )
    order = jnp.stack([quarter(1 - x, 1 - s), between[0], between[1], quarter(x, s)])
    sent, kept = merge_partial(order.astype(jnp.int32), tokens, merger_weight, other_rows)
    kept = kept + swap(sent, first_hop).astype(jnp.float32)
    received = swap(kept[:half].astype(jnp.bfloat16), second_hop)

    block_places = []
    for core_step in range(2):
        owner = c ^ core_step
        for far_step in range(2):
            for hop_step in range(2):
                kind = x ^ jnp.where(owner == 0, hop_step, far_step)
                owner_seq = s ^ jnp.where(owner == 0, far_step, hop_step)
                block_places += [owner * seqs + owner_seq, kind]
    payload = project_visual(
        jnp.stack(block_places).astype(jnp.int32), kept[half:], received, lm_norm_gain, kv_blocks, tps
    )
    visual = finish_visual(exchange(payload, "tp"), half)
    twin = swap(visual, other_seq)

    places = jnp.stack([patch_total // 4, s * half, (1 - s) * half]).astype(jnp.int32)
    return prompt_visual(places, queries[0], visual, twin, near, half)[None]


def solution(mesh):
    sizes = dict(mesh.shape)
    images, seqs, tps = (sizes[name] for name in ("img", "seq", "tp"))
    suited = (
        images == 4
        and seqs == 2
        and images * seqs == 2 * tps
        and VIT_HEADS % (seqs * tps) == 0
        and KVH % tps == 0
    )
    if not suited:
        placed = (
            P("img", ("seq", "tp"), None, None),
            P("img"),
            P(),
            P(),
            P(("img", "seq"), "tp"),
            P("tp"),
            P("tp", ("img", "seq")),
            P("img", "seq", "tp", None),
            P("img", "seq", None, "tp", None),
        )
        return jax.shard_map(
            local, mesh=mesh, in_specs=placed, out_specs=P("img", "seq", "tp", None), check_vma=False
        )
    split = Mesh(
        mesh.devices.reshape(images // 2, 2, seqs, tps), ("x", "c", "seq", "tp")
    )
    image = ("x", "c")
    placed = (
        P(image, ("seq", "tp"), None, None),
        P(image),
        P(),
        P(),
        P(("x", "c", "seq"), "tp"),
        P("tp"),
        P("tp", ("x", "c", "seq")),
        P(image, "seq", "tp", None),
        P(image, "seq", None, "tp", None),
    )
    return jax.shard_map(
        fast_local, mesh=split, in_specs=placed, out_specs=P(image, "seq", "tp", None), check_vma=False
    )
```

```python
import math

import jax
import jax.numpy as jnp
from jax import lax
from jax.experimental import pallas as pl
from jax.experimental.pallas import tpu as pltpu
from jax.sharding import Mesh
from jax.sharding import PartitionSpec as P

VIT_D = 1280
VIT_HEADS = 16
VIT_HDIM = 80
D = 8192
HQ = 64
KVH = 8
HD = 128


masked_score = -1e30
LOG2E = math.log2(math.e)


def fold_block(running, scores, usable, value_block, forms):
    peak, weight_sum, blended = running
    scores = jnp.where(usable, scores, masked_score)
    new_peak = jnp.maximum(peak, jnp.max(scores, axis=-1))
    weights = jnp.where(usable, jnp.exp(scores - new_peak[..., None]), 0.0)
    decay = jnp.exp(peak - new_peak)
    weight_sum = weight_sum * decay + jnp.sum(weights, axis=-1)
    blended = blended * decay[..., None] + jnp.einsum(
        forms, weights.astype(jnp.bfloat16), value_block, preferred_element_type=jnp.float32
    )
    return (new_peak, weight_sum, blended)


def local(
    vit_qkv,
    patch_counts,
    vit_out_weight,
    vit_norm_gain,
    merger_weight,
    lm_norm_gain,
    kv_weight,
    queries,
    span_kv,
):
    patch_rows = vit_qkv.shape[1]
    tp_count = lax.axis_size("tp")
    seq_index = lax.axis_index("seq")
    tp_index = lax.axis_index("tp")
    patch_total = patch_counts[0]
    local_qkv = vit_qkv[0].reshape(patch_rows, 3, VIT_HEADS, VIT_HDIM)
    scaling = VIT_HDIM ** (-0.5)
    spread = lax.all_to_all(local_qkv, "seq", split_axis=2, concat_axis=0, tiled=True)
    local_rows = spread.shape[0]

    def seq_rows(index):
        source = index // local_rows
        within = index % local_rows
        return (within // patch_rows * tp_count + source) * patch_rows + within % patch_rows

    heads_local = spread.shape[2]
    query_count = spread.shape[0]
    query_rows = spread[:, 0]
    running = (
        jnp.full((heads_local, query_count), masked_score, jnp.float32),
        jnp.zeros((heads_local, query_count), jnp.float32),
        jnp.zeros((heads_local, query_count, VIT_HDIM), jnp.float32),
    )
    make_heads_local = query_rows.shape[1]
    key_piece = lax.all_gather(spread[:, 1], "tp", axis=0, tiled=True)
    value_piece = lax.all_gather(spread[:, 2], "tp", axis=0, tiled=True)
    blocks = key_piece.shape[0] // local_rows
    key_blocks = key_piece.reshape(blocks, local_rows, make_heads_local, VIT_HDIM)
    value_blocks = value_piece.reshape(blocks, local_rows, make_heads_local, VIT_HDIM)
    offsets = jnp.arange(blocks, dtype=jnp.int32) * local_rows

    def make_advance(state, inputs):
        key_block, value_block, offset = inputs
        usable = seq_rows(offset + jnp.arange(local_rows, dtype=jnp.int32)) < patch_total
        scores = (
            jnp.einsum("qhd,khd->hqk", query_rows, key_block, preferred_element_type=jnp.float32)
            * scaling
        )
        return (fold_block(state, scores, usable[None, None, :], value_block, "hqk,khd->hqd"), None)

    result, _ = lax.scan(make_advance, running, (key_blocks, value_blocks, offsets))
    state = result
    peak, weight_sum, blended = state
    returned = lax.all_to_all(
        jnp.transpose(blended / weight_sum[..., None], (1, 0, 2)).astype(jnp.bfloat16),
        "seq",
        split_axis=0,
        concat_axis=1,
        tiled=True,
    )
    attended = returned.reshape(patch_rows, VIT_D)
    hidden = jnp.dot(attended, vit_out_weight, preferred_element_type=jnp.float32)
    patch_ids = (seq_index * tp_count + tp_index) * patch_rows + jnp.arange(
        patch_rows, dtype=jnp.int32
    )
    hidden = jnp.where((patch_ids < patch_total)[:, None], hidden, 0.0)
    centred = hidden - jnp.mean(hidden, axis=-1, keepdims=True)
    spread_sq = jnp.mean(centred * centred, axis=-1, keepdims=True)
    normed = (centred * lax.rsqrt(spread_sq + 1e-06) * vit_norm_gain).astype(jnp.bfloat16)
    merged_local = normed.reshape(patch_rows // 4, 4 * VIT_D)
    token_rows = lax.all_gather(merged_local, "tp", axis=0, tiled=True)
    embedded_sum = jnp.dot(
        token_rows,
        lax.all_gather(merger_weight, ("img", "seq"), axis=0, tiled=True),
        preferred_element_type=jnp.float32,
    )
    embedded = lax.optimization_barrier(embedded_sum.astype(jnp.bfloat16))
    embedded_wide = embedded.astype(jnp.float32)
    square_sums = lax.psum(jnp.sum(embedded_wide * embedded_wide, axis=-1), "tp")
    lm_normed = (embedded_wide * lax.rsqrt(square_sums[:, None] / D + 1e-06) * lm_norm_gain).astype(
        jnp.bfloat16
    )
    kv_terms = jnp.dot(
        lm_normed,
        lax.all_gather(kv_weight, ("img", "seq"), axis=1, tiled=True),
        preferred_element_type=jnp.float32,
    )
    visual_count = kv_terms.shape[0]
    kv_terms = kv_terms.reshape(visual_count, 2, KVH, HD)
    visual_kv = lax.psum_scatter(
        kv_terms.astype(jnp.bfloat16), "tp", scatter_dimension=2, tiled=True
    )
    span_rows = queries.shape[1]
    kv_local = span_kv.shape[3]
    groups = HQ // KVH
    lm_scaling = HD ** (-0.5)
    grouped = queries[0].reshape(span_rows, kv_local, groups, HD)
    causal = jnp.arange(span_rows)[:, None] >= jnp.arange(span_rows)[None, :]
    near_scores = (
        jnp.einsum("ckgd,nkd->kgcn", grouped, span_kv[0, :, 0], preferred_element_type=jnp.float32)
        * lm_scaling
    )
    initial = (
        jnp.full((kv_local, groups, span_rows), masked_score, jnp.float32),
        jnp.zeros((kv_local, groups, span_rows), jnp.float32),
        jnp.zeros((kv_local, groups, span_rows, HD), jnp.float32),
    )
    initial = fold_block(
        initial, near_scores, causal[None, None], span_kv[0, :, 1], "kgcn,nkd->kgcd"
    )
    visual_total = patch_total // 4
    key_piece = lax.all_gather(visual_kv[:, 0], "seq", axis=0, tiled=True)
    value_piece = lax.all_gather(visual_kv[:, 1], "seq", axis=0, tiled=True)
    blocks = key_piece.shape[0] // visual_count
    key_blocks = key_piece.reshape(blocks, visual_count, kv_local, HD)
    value_blocks = value_piece.reshape(blocks, visual_count, kv_local, HD)
    offsets = jnp.arange(blocks, dtype=jnp.int32) * visual_count

    def visual_advance(state, inputs):
        key_block, value_block, offset = inputs
        usable = offset + jnp.arange(visual_count, dtype=jnp.int32) < visual_total
        scores = (
            jnp.einsum("ckgd,nkd->kgcn", grouped, key_block, preferred_element_type=jnp.float32)
            * lm_scaling
        )
        return (
            fold_block(state, scores, usable[None, None, None, :], value_block, "kgcn,nkd->kgcd"),
            None,
        )

    result, _ = lax.scan(visual_advance, initial, (key_blocks, value_blocks, offsets))
    peak, weight_sum, blended = result
    result = jnp.transpose(blended / weight_sum[..., None], (2, 0, 1, 3))
    return result.reshape(span_rows, kv_local * groups, HD).astype(jnp.bfloat16)[None]


def whole(*arrays):
    return [pl.BlockSpec(memory_space=pltpu.SMEM if a.dtype == jnp.int32 else pltpu.VMEM) for a in arrays]


def onchip(array):
    return pltpu.with_memory_space_constraint(array, pltpu.VMEM)


def offchip(array):
    return pltpu.with_memory_space_constraint(array, pltpu.HBM)


def grant(mib):
    return pltpu.CompilerParams(vmem_limit_bytes=mib << 20)


def call(body, outs, *arrays, scratch=(), stay=(), mib=12):
    arrays = [onchip(a) if k in stay else a for k, a in enumerate(arrays)]
    return pl.pallas_call(
        body,
        out_shape=outs,
        in_specs=whole(*arrays),
        out_specs=jax.tree.map(lambda _: pl.BlockSpec(memory_space=pltpu.VMEM), outs),
        scratch_shapes=list(scratch),
        compiler_params=grant(mib),
    )(*arrays)


def pack_heads(rows, owners):
    kinds, patches, width = rows.shape
    share = width // owners

    def body(rows_ref, out_ref):
        for kind in range(kinds):
            values = rows_ref[kind]
            for owner in range(owners):
                out_ref[owner, :, kind * share : (kind + 1) * share] = values[
                    :, owner * share : (owner + 1) * share
                ]

    return call(body, jax.ShapeDtypeStruct((owners, patches, kinds * share), rows.dtype), rows)


def vision_attention(spread, scalars):
    owners, patches, width = spread.shape
    share = width // 3
    heads = share // VIT_HDIM
    slots = owners * patches
    block = 128
    lanes = 128
    tail = share - lanes
    folds = lanes // tail
    tail_rows = patches // folds
    factor = VIT_HDIM ** (-0.5) * LOG2E

    def body(scalars_ref, spread_ref, out_ref):
        values = spread_ref[...].reshape(slots, width)
        keys = values[:, share : 2 * share]
        last = values[:, 2 * share :]
        usable = lax.broadcasted_iota(jnp.int32, (1, slots), 1) < scalars_ref[0]
        lane_head = lax.broadcasted_iota(jnp.int32, (1, share), 1) // VIT_HDIM
        for start in range(0, slots, block):
            query = values[start : start + block, :share]
            result = jnp.zeros((block, share), jnp.float32)
            for head in range(heads):
                own = lane_head == head
                picked = jnp.where(own, query, jnp.zeros_like(query))
                scores = lax.dot_general(
                    picked, keys, (((1,), (1,)), ((), ())), preferred_element_type=jnp.float32
                )
                scores = jnp.where(usable, scores, masked_score)
                peak = jnp.max(scores, axis=-1, keepdims=True)
                weights = jnp.exp2((scores - peak) * factor)
                weight_sum = jnp.sum(weights, axis=-1, keepdims=True)
                blended = jnp.dot(
                    weights.astype(jnp.bfloat16), last, preferred_element_type=jnp.float32
                )
                result = jnp.where(own, blended / weight_sum, result)
            for part in range(block // patches):
                piece = result[part * patches : (part + 1) * patches]
                owner = start // patches + part
                out_ref[owner, :patches, :] = piece[:, :lanes].astype(jnp.bfloat16)
                out_ref[owner, patches:, :] = jnp.concatenate(
                    [piece[k * tail_rows : (k + 1) * tail_rows, lanes:] for k in range(folds)], axis=1
                ).astype(jnp.bfloat16)

    out = jax.ShapeDtypeStruct((owners, patches + tail_rows, lanes), jnp.bfloat16)
    return call(body, out, scalars, spread, stay=(1,))


def project_norm(scalars, returned, out_weight, gain, plane, seqs, tps, rows_local):
    owners, packed_rows, lanes = returned.shape
    width = out_weight.shape[0]
    share = width // owners
    tail = share - lanes
    folds = lanes // tail
    patches = packed_rows * folds // (folds + 1)
    token_rows = patches // 4
    tiles = width // lanes

    def body(scalars_ref, returned_ref, weight_ref, gain_ref, out_ref, rows_ref):
        pieces = []
        for owner in range(owners):
            pieces.append(returned_ref[owner, :patches, :].astype(jnp.float32))
            rest = returned_ref[owner, patches:, :].astype(jnp.float32)
            pieces.append(
                jnp.concatenate([rest[:, k * tail : (k + 1) * tail] for k in range(folds)], axis=0)
            )
        attended = jnp.concatenate(pieces, axis=1).astype(jnp.bfloat16)
        hidden = jnp.dot(attended, weight_ref[...], preferred_element_type=jnp.float32)
        ids = lax.broadcasted_iota(jnp.int32, (patches, 1), 0) + scalars_ref[1]
        hidden = jnp.where(ids < scalars_ref[0], hidden, 0.0)
        centred = hidden - jnp.mean(hidden, axis=-1, keepdims=True)
        spread_sq = jnp.mean(centred * centred, axis=-1, keepdims=True)
        normed = centred * lax.rsqrt(spread_sq + 1e-06) * gain_ref[...]
        for tile in range(tiles):
            rows_ref[tile] = normed[:, tile * lanes : (tile + 1) * lanes]
        even = scalars_ref[2] == 0
        for xq in range(plane):
            pair = [
                jnp.concatenate(
                    [
                        rows_ref[tile, pl.ds(2 * xq + core, token_rows, stride=4), :]
                        for tile in range(tiles)
                    ],
                    axis=1,
                ).astype(jnp.bfloat16)
                for core in range(2)
            ]
            first = jnp.where(even, pair[0], pair[1])
            second = jnp.where(even, pair[1], pair[0])
            for sq in range(seqs):
                for tq in range(tps):
                    place = (xq * seqs + sq) * tps + tq
                    cut = slice(sq * rows_local, (sq + 1) * rows_local)
                    out_ref[place, :, :rows_local] = first[:, cut]
                    out_ref[place, :, rows_local:] = second[:, cut]

    out = jax.ShapeDtypeStruct((plane * seqs * tps, token_rows, 2 * rows_local), jnp.bfloat16)
    return call(
        body, out, scalars, returned, out_weight, gain[None],
        scratch=[pltpu.VMEM((tiles, patches, lanes), jnp.float32)],
        stay=(1,), mib=16,
    )


def merge_partial(scalars, tokens, own_weight, other_weight):
    quarters, half, depth = tokens.shape
    rows_local, columns = own_weight.shape
    block = 512

    def body(scalars_ref, tokens_ref, own_ref, other_ref, sent_ref, kept_ref):
        rows = jnp.concatenate([tokens_ref[scalars_ref[3 + k]] for k in range(quarters)], axis=0)
        result = jnp.dot(rows[:, :rows_local], own_ref[...], preferred_element_type=jnp.float32)
        result = result + jnp.dot(
            rows[:, rows_local:], other_ref[...], preferred_element_type=jnp.float32
        )
        sent_ref[...] = result[: 2 * half].astype(jnp.bfloat16)
        kept_ref[...] = result[2 * half :]

    weight_spec = pl.BlockSpec((rows_local, block), lambda n: (0, n))
    out_spec = pl.BlockSpec((2 * half, block), lambda n: (0, n))
    return pl.pallas_call(
        body,
        grid=(columns // block,),
        out_shape=(
            jax.ShapeDtypeStruct((2 * half, columns), jnp.bfloat16),
            jax.ShapeDtypeStruct((2 * half, columns), jnp.float32),
        ),
        in_specs=[
            pl.BlockSpec(memory_space=pltpu.SMEM),
            pl.BlockSpec((quarters, half, depth), lambda n: (0, 0, 0)),
            weight_spec,
            weight_spec,
        ],
        out_specs=(out_spec, out_spec),
        compiler_params=grant(24),
    )(scalars, onchip(tokens), offchip(own_weight), offchip(other_weight))


def add_received(kept, received):
    half = kept.shape[0] // 2

    def body(kept_ref, received_ref, sent_ref, out_ref):
        result = kept_ref[...] + received_ref[...].astype(jnp.float32)
        sent_ref[...] = result[:half].astype(jnp.bfloat16)
        out_ref[...] = result[half:]

    outs = (
        jax.ShapeDtypeStruct((half, kept.shape[1]), jnp.bfloat16),
        jax.ShapeDtypeStruct((half, kept.shape[1]), jnp.float32),
    )
    return call(body, outs, kept, received, stay=(0, 1))


def project_visual(scalars, kept, received, gain, blocks, tps):
    half, depth = kept.shape
    width = blocks[0].shape[1]
    count = len(blocks)
    extra = 16

    def body(scalars_ref, kept_ref, received_ref, gain_ref, *refs):
        block_refs, out_ref = refs[:count], refs[count]
        buffers, sems = refs[count + 1 :]
        copies = [
            pltpu.make_async_copy(block_refs[k], buffers.at[k], sems.at[k]) for k in range(count)
        ]
        for copy in copies:
            copy.start()
        embedded = kept_ref[...] + received_ref[...].astype(jnp.float32)
        squares = jnp.sum(embedded * embedded, axis=-1, keepdims=True)
        gained = (embedded * gain_ref[...]).astype(jnp.bfloat16)
        flat = jnp.broadcast_to(squares, (half, 128)).T[:extra]
        coarse = flat.astype(jnp.bfloat16).astype(jnp.float32)
        upper = lax.broadcasted_iota(jnp.int32, (extra, half), 0) < extra // 2
        both = jnp.where(upper, coarse, flat - coarse)
        both = jnp.concatenate([both, jnp.zeros((extra, width - half), jnp.float32)], axis=1)
        both = both.astype(jnp.bfloat16)
        for dest in range(tps):
            out_ref[dest, 2 * half :, :] = both
        for k in range(count):
            copies[k].wait()
            term = jnp.dot(gained, buffers[k], preferred_element_type=jnp.float32)
            row = pl.multiple_of(scalars_ref[11 + 2 * k] * half, half)
            out_ref[scalars_ref[10 + 2 * k], pl.ds(row, half), :] = term.astype(jnp.bfloat16)

    out = jax.ShapeDtypeStruct((tps, 2 * half + extra, width), jnp.bfloat16)
    return pl.pallas_call(
        body,
        out_shape=out,
        in_specs=[pl.BlockSpec(memory_space=pltpu.SMEM)]
        + [pl.BlockSpec(memory_space=pltpu.VMEM)] * 3
        + [pl.BlockSpec(memory_space=pl.ANY)] * count,
        out_specs=pl.BlockSpec(memory_space=pltpu.VMEM),
        scratch_shapes=[
            pltpu.VMEM((count, depth, width), jnp.bfloat16),
            pltpu.SemaphoreType.DMA((count,)),
        ],
        compiler_params=grant(24),
    )(scalars, onchip(kept), onchip(received), gain[None], *[offchip(block) for block in blocks])


def finish_visual(sums, half):
    width = sums.shape[2]

    def body(sums_ref, out_ref):
        total = jnp.sum(sums_ref[...].astype(jnp.float32), axis=0)
        flat = total[2 * half : 2 * half + 8] + total[2 * half + 8 :]
        squares = jnp.broadcast_to(flat[:1, :128], (128, 128)).T[:half, :1]
        scale = lax.rsqrt(squares / D + 1e-06)
        out_ref[:half] = (total[:half] * scale).astype(jnp.bfloat16)
        out_ref[half:] = (total[half : 2 * half] * scale).astype(jnp.bfloat16)

    return call(body, jax.ShapeDtypeStruct((2 * half, width), jnp.bfloat16), sums, stay=(0,))


def split_queries(block, kv_local):
    tokens, heads, width = block.shape
    groups = heads // kv_local
    wide = block.astype(jnp.float32).reshape(tokens, kv_local, groups, width)
    return [
        wide[:, k].reshape(tokens * groups, width).astype(jnp.bfloat16) for k in range(kv_local)
    ]


def prompt_own(queries, span_kv, kv_head):
    tokens, heads, width = queries.shape
    kv_local = span_kv.shape[2]
    groups = heads // kv_local
    block = 128
    rows = block * groups
    factor = HD ** (-0.5) * LOG2E

    def body(queries_ref, span_ref, out_ref, stats_ref):
        every_key = span_ref[:, 0, kv_head, :]
        every_value = span_ref[:, 1, kv_head, :]
        for index in range(tokens // block):
            start = index * block
            query = split_queries(queries_ref[start : start + block], kv_local)[kv_head]
            extent = start + block
            keys = every_key[:extent]
            values = every_value[:extent]
            scores = lax.dot_general(
                keys, query, (((1,), (1,)), ((), ())), preferred_element_type=jnp.float32
            )
            key_ids = lax.broadcasted_iota(jnp.int32, (extent, rows), 0)
            token_ids = start + lax.broadcasted_iota(jnp.int32, (extent, rows), 1) // groups
            scores = jnp.where(key_ids <= token_ids, scores, masked_score)
            peak = jnp.max(scores, axis=0, keepdims=True)
            weights = jnp.exp2((scores - peak) * factor)
            cut = slice(start * groups, extent * groups)
            stats_ref[0:1, cut] = peak
            stats_ref[1:2, cut] = jnp.sum(weights, axis=0, keepdims=True)
            out_ref[:, cut] = lax.dot_general(
                values, weights.astype(jnp.bfloat16), (((0,), (0,)), ((), ())),
                preferred_element_type=jnp.float32,
            )

    outs = (
        jax.ShapeDtypeStruct((width, tokens * groups), jnp.float32),
        jax.ShapeDtypeStruct((2, tokens * groups), jnp.float32),
    )
    return call(body, outs, offchip(queries), offchip(span_kv), mib=24)


def prompt_visual(scalars, queries, own, twin, near, half):
    tokens, heads, width = queries.shape
    kv_local = len(near)
    groups = heads // kv_local
    block = 128
    rows = block * groups
    factor = HD ** (-0.5) * LOG2E

    def body(scalars_ref, queries_ref, own_ref, twin_ref, *refs):
        near_refs, out_ref = refs[:-1], refs[-1]
        split = split_queries(queries_ref[...], kv_local)
        ids = lax.broadcasted_iota(jnp.int32, (2 * half, 1), 0)
        ids = jnp.where(ids < half, ids + scalars_ref[8], ids - half + scalars_ref[9])
        seen = ids < scalars_ref[7]
        results = []
        for k in range(kv_local):
            cut = slice(k * width, (k + 1) * width)
            keys = jnp.concatenate([own_ref[:half, cut], twin_ref[:half, cut]], axis=0)
            values = jnp.concatenate([own_ref[half:, cut], twin_ref[half:, cut]], axis=0)
            scores = lax.dot_general(
                keys, split[k], (((1,), (1,)), ((), ())), preferred_element_type=jnp.float32
            )
            scores = jnp.where(seen, scores, masked_score)
            stats = near_refs[2 * k + 1][...]
            peak = jnp.maximum(stats[0:1], jnp.max(scores, axis=0, keepdims=True))
            weights = jnp.exp2((scores - peak) * factor)
            decay = jnp.exp2((stats[0:1] - peak) * factor)
            total = stats[1:2] * decay + jnp.sum(weights, axis=0, keepdims=True)
            blended = lax.dot_general(
                values, weights.astype(jnp.bfloat16), (((0,), (0,)), ((), ())),
                preferred_element_type=jnp.float32,
            )
            blended = (blended + near_refs[2 * k][...] * decay) / total
            results.append(blended.T.reshape(block, 1, groups, width))
        joined = jnp.concatenate(results, axis=1).reshape(block, heads, width)
        out_ref[...] = joined.astype(jnp.bfloat16)

    query_spec = pl.BlockSpec((block, heads, width), lambda n: (n, 0, 0))
    fixed = pl.BlockSpec((2 * half, kv_local * width), lambda n: (0, 0))
    near_specs = [
        pl.BlockSpec((width, rows), lambda n: (0, n)),
        pl.BlockSpec((2, rows), lambda n: (0, n)),
    ] * kv_local
    return pl.pallas_call(
        body,
        grid=(tokens // block,),
        out_shape=jax.ShapeDtypeStruct(queries.shape, jnp.bfloat16),
        in_specs=[pl.BlockSpec(memory_space=pltpu.SMEM), query_spec, fixed, fixed] + near_specs,
        out_specs=query_spec,
        compiler_params=grant(24),
    )(scalars, offchip(queries), onchip(own), onchip(twin), *[offchip(part) for pair in near for part in pair])


def swap_pairs(plane, seqs, tps, move):
    pairs = []
    for x in range(plane):
        for c in range(2):
            for s in range(seqs):
                for t in range(tps):
                    x2, c2, s2 = move(x, c, s)
                    pairs.append((((x * 2 + c) * seqs + s) * tps + t, ((x2 * 2 + c2) * seqs + s2) * tps + t))
    return pairs


def fast_local(
    vit_qkv,
    patch_counts,
    vit_out_weight,
    vit_norm_gain,
    merger_weight,
    lm_norm_gain,
    kv_weight,
    queries,
    span_kv,
):
    everything = ("x", "c", "seq", "tp")
    plane = lax.axis_size("x")
    seqs = lax.axis_size("seq")
    tps = lax.axis_size("tp")
    x, c, s, t = (lax.axis_index(name) for name in everything)
    owners = seqs * tps
    patch_rows = vit_qkv.shape[1]
    token_rows = patch_rows // 4
    half = tps * token_rows
    rows_local = merger_weight.shape[0]
    patch_total = patch_counts[0]

    def swap(value, move):
        return lax.ppermute(value, everything, swap_pairs(plane, seqs, tps, move))

    def exchange(value, names):
        return lax.all_to_all(value, names, split_axis=0, concat_axis=0, tiled=True)

    def other_core(x, c, s):
        return x, 1 - c, s

    def first_hop(x, c, s):
        return (1 - x, c, s) if c == 0 else (x, c, 1 - s)

    def second_hop(x, c, s):
        return (x, c, 1 - s) if c == 0 else (1 - x, c, s)

    def other_seq(x, c, s):
        return x, c, 1 - s

    def quarter(xq, sq):
        return xq * seqs + sq

    even = c == 0
    scalars = [patch_total, (s * tps + t) * patch_rows, c, quarter(1 - x, 1 - s)]
    scalars.append(jnp.where(even, quarter(1 - x, s), quarter(x, 1 - s)))
    scalars.append(jnp.where(even, quarter(x, 1 - s), quarter(1 - x, s)))
    scalars += [quarter(x, s), patch_total // 4, s * half, (1 - s) * half]
    for core_step in range(2):
        owner = c ^ core_step
        for far_step in range(2):
            for hop_step in range(2):
                owner_seq = s ^ jnp.where(owner == 0, far_step, hop_step)
                scalars += [owner * seqs + owner_seq, x ^ jnp.where(owner == 0, hop_step, far_step)]
    scalars = jnp.stack(scalars).astype(jnp.int32)

    other_rows = swap(merger_weight, other_core)
    packed = pack_heads(jnp.transpose(vit_qkv[0], (1, 0, 2)), owners)
    spread = exchange(packed, ("seq", "tp"))

    near_block = swap(kv_weight, first_hop)
    side_block = swap(kv_weight, second_hop)
    far_block = swap(near_block, second_hop)
    chip_blocks = [kv_weight, near_block, side_block, far_block]
    kv_blocks = list(chip_blocks)
    for block in chip_blocks:
        kv_blocks.append(swap(block, other_core))

    near = []
    for k in range(span_kv.shape[3]):
        near.append(prompt_own(queries[0], span_kv[0], k))

    attended = vision_attention(spread, scalars)
    returned = exchange(attended, ("seq", "tp"))
    merged = project_norm(
        scalars, returned, vit_out_weight, vit_norm_gain, plane, seqs, tps, rows_local
    )

    tokens = exchange(merged, ("x", "seq", "tp")).reshape(plane * seqs, half, 2 * rows_local)
    sent, kept = merge_partial(scalars, tokens, merger_weight, other_rows)
    received = swap(sent, first_hop)
    sent, kept = add_received(kept, received)
    received = swap(sent, second_hop)

    payload = project_visual(scalars, kept, received, lm_norm_gain, kv_blocks, tps)
    sums = exchange(payload, "tp")
    visual = finish_visual(sums, half)
    twin = swap(visual, other_seq)

    return prompt_visual(scalars, queries[0], visual, twin, near, half)[None]


def solution(mesh):
    sizes = dict(mesh.shape)
    images, seqs, tps = (sizes[name] for name in ("img", "seq", "tp"))
    suited = (
        images == 4
        and seqs == 2
        and images * seqs == 2 * tps
        and VIT_HEADS % (seqs * tps) == 0
        and KVH % tps == 0
    )
    if not suited:
        placed = (
            P("img", ("seq", "tp"), None, None),
            P("img"),
            P(),
            P(),
            P(("img", "seq"), "tp"),
            P("tp"),
            P("tp", ("img", "seq")),
            P("img", "seq", "tp", None),
            P("img", "seq", None, "tp", None),
        )
        return jax.shard_map(
            local, mesh=mesh, in_specs=placed, out_specs=P("img", "seq", "tp", None), check_vma=False
        )
    split = Mesh(
        mesh.devices.reshape(images // 2, 2, seqs, tps), ("x", "c", "seq", "tp")
    )
    image = ("x", "c")
    placed = (
        P(image, ("seq", "tp"), None, None),
        P(image),
        P(),
        P(),
        P(("x", "c", "seq"), "tp"),
        P("tp"),
        P("tp", ("x", "c", "seq")),
        P(image, "seq", "tp", None),
        P(image, "seq", None, "tp", None),
    )

    return jax.shard_map(
        fast_local, mesh=split, in_specs=placed, out_specs=P(image, "seq", "tp", None), check_vma=False
    )
```

```python
import math

import jax
import jax.numpy as jnp
from jax import lax
from jax.experimental import pallas as pl
from jax.experimental.pallas import tpu as pltpu
from jax.sharding import Mesh
from jax.sharding import PartitionSpec as P

VIT_D = 1280
VIT_HEADS = 16
VIT_HDIM = 80
D = 8192
HQ = 64
KVH = 8
HD = 128


masked_score = -1e30
LOG2E = math.log2(math.e)


def fold_block(running, scores, usable, value_block, forms):
    peak, weight_sum, blended = running
    scores = jnp.where(usable, scores, masked_score)
    new_peak = jnp.maximum(peak, jnp.max(scores, axis=-1))
    weights = jnp.where(usable, jnp.exp(scores - new_peak[..., None]), 0.0)
    decay = jnp.exp(peak - new_peak)
    weight_sum = weight_sum * decay + jnp.sum(weights, axis=-1)
    blended = blended * decay[..., None] + jnp.einsum(
        forms, weights.astype(jnp.bfloat16), value_block, preferred_element_type=jnp.float32
    )
    return (new_peak, weight_sum, blended)


def local(
    vit_qkv,
    patch_counts,
    vit_out_weight,
    vit_norm_gain,
    merger_weight,
    lm_norm_gain,
    kv_weight,
    queries,
    span_kv,
):
    patch_rows = vit_qkv.shape[1]
    tp_count = lax.axis_size("tp")
    seq_index = lax.axis_index("seq")
    tp_index = lax.axis_index("tp")
    patch_total = patch_counts[0]
    local_qkv = vit_qkv[0].reshape(patch_rows, 3, VIT_HEADS, VIT_HDIM)
    scaling = VIT_HDIM ** (-0.5)
    spread = lax.all_to_all(local_qkv, "seq", split_axis=2, concat_axis=0, tiled=True)
    local_rows = spread.shape[0]

    def seq_rows(index):
        source = index // local_rows
        within = index % local_rows
        return (within // patch_rows * tp_count + source) * patch_rows + within % patch_rows

    heads_local = spread.shape[2]
    query_count = spread.shape[0]
    query_rows = spread[:, 0]
    running = (
        jnp.full((heads_local, query_count), masked_score, jnp.float32),
        jnp.zeros((heads_local, query_count), jnp.float32),
        jnp.zeros((heads_local, query_count, VIT_HDIM), jnp.float32),
    )
    make_heads_local = query_rows.shape[1]
    key_piece = lax.all_gather(spread[:, 1], "tp", axis=0, tiled=True)
    value_piece = lax.all_gather(spread[:, 2], "tp", axis=0, tiled=True)
    blocks = key_piece.shape[0] // local_rows
    key_blocks = key_piece.reshape(blocks, local_rows, make_heads_local, VIT_HDIM)
    value_blocks = value_piece.reshape(blocks, local_rows, make_heads_local, VIT_HDIM)
    offsets = jnp.arange(blocks, dtype=jnp.int32) * local_rows

    def make_advance(state, inputs):
        key_block, value_block, offset = inputs
        usable = seq_rows(offset + jnp.arange(local_rows, dtype=jnp.int32)) < patch_total
        scores = (
            jnp.einsum("qhd,khd->hqk", query_rows, key_block, preferred_element_type=jnp.float32)
            * scaling
        )
        return (fold_block(state, scores, usable[None, None, :], value_block, "hqk,khd->hqd"), None)

    result, _ = lax.scan(make_advance, running, (key_blocks, value_blocks, offsets))
    state = result
    peak, weight_sum, blended = state
    returned = lax.all_to_all(
        jnp.transpose(blended / weight_sum[..., None], (1, 0, 2)).astype(jnp.bfloat16),
        "seq",
        split_axis=0,
        concat_axis=1,
        tiled=True,
    )
    attended = returned.reshape(patch_rows, VIT_D)
    hidden = jnp.dot(attended, vit_out_weight, preferred_element_type=jnp.float32)
    patch_ids = (seq_index * tp_count + tp_index) * patch_rows + jnp.arange(
        patch_rows, dtype=jnp.int32
    )
    hidden = jnp.where((patch_ids < patch_total)[:, None], hidden, 0.0)
    centred = hidden - jnp.mean(hidden, axis=-1, keepdims=True)
    spread_sq = jnp.mean(centred * centred, axis=-1, keepdims=True)
    normed = (centred * lax.rsqrt(spread_sq + 1e-06) * vit_norm_gain).astype(jnp.bfloat16)
    merged_local = normed.reshape(patch_rows // 4, 4 * VIT_D)
    token_rows = lax.all_gather(merged_local, "tp", axis=0, tiled=True)
    embedded_sum = jnp.dot(
        token_rows,
        lax.all_gather(merger_weight, ("img", "seq"), axis=0, tiled=True),
        preferred_element_type=jnp.float32,
    )
    embedded = lax.optimization_barrier(embedded_sum.astype(jnp.bfloat16))
    embedded_wide = embedded.astype(jnp.float32)
    square_sums = lax.psum(jnp.sum(embedded_wide * embedded_wide, axis=-1), "tp")
    lm_normed = (embedded_wide * lax.rsqrt(square_sums[:, None] / D + 1e-06) * lm_norm_gain).astype(
        jnp.bfloat16
    )
    kv_terms = jnp.dot(
        lm_normed,
        lax.all_gather(kv_weight, ("img", "seq"), axis=1, tiled=True),
        preferred_element_type=jnp.float32,
    )
    visual_count = kv_terms.shape[0]
    kv_terms = kv_terms.reshape(visual_count, 2, KVH, HD)
    visual_kv = lax.psum_scatter(
        kv_terms.astype(jnp.bfloat16), "tp", scatter_dimension=2, tiled=True
    )
    span_rows = queries.shape[1]
    kv_local = span_kv.shape[3]
    groups = HQ // KVH
    lm_scaling = HD ** (-0.5)
    grouped = queries[0].reshape(span_rows, kv_local, groups, HD)
    causal = jnp.arange(span_rows)[:, None] >= jnp.arange(span_rows)[None, :]
    near_scores = (
        jnp.einsum("ckgd,nkd->kgcn", grouped, span_kv[0, :, 0], preferred_element_type=jnp.float32)
        * lm_scaling
    )
    initial = (
        jnp.full((kv_local, groups, span_rows), masked_score, jnp.float32),
        jnp.zeros((kv_local, groups, span_rows), jnp.float32),
        jnp.zeros((kv_local, groups, span_rows, HD), jnp.float32),
    )
    initial = fold_block(
        initial, near_scores, causal[None, None], span_kv[0, :, 1], "kgcn,nkd->kgcd"
    )
    visual_total = patch_total // 4
    key_piece = lax.all_gather(visual_kv[:, 0], "seq", axis=0, tiled=True)
    value_piece = lax.all_gather(visual_kv[:, 1], "seq", axis=0, tiled=True)
    blocks = key_piece.shape[0] // visual_count
    key_blocks = key_piece.reshape(blocks, visual_count, kv_local, HD)
    value_blocks = value_piece.reshape(blocks, visual_count, kv_local, HD)
    offsets = jnp.arange(blocks, dtype=jnp.int32) * visual_count

    def visual_advance(state, inputs):
        key_block, value_block, offset = inputs
        usable = offset + jnp.arange(visual_count, dtype=jnp.int32) < visual_total
        scores = (
            jnp.einsum("ckgd,nkd->kgcn", grouped, key_block, preferred_element_type=jnp.float32)
            * lm_scaling
        )
        return (
            fold_block(state, scores, usable[None, None, None, :], value_block, "kgcn,nkd->kgcd"),
            None,
        )

    result, _ = lax.scan(visual_advance, initial, (key_blocks, value_blocks, offsets))
    peak, weight_sum, blended = result
    result = jnp.transpose(blended / weight_sum[..., None], (2, 0, 1, 3))
    return result.reshape(span_rows, kv_local * groups, HD).astype(jnp.bfloat16)[None]


def whole(*arrays):
    return [pl.BlockSpec(memory_space=pltpu.SMEM if a.dtype == jnp.int32 else pltpu.VMEM) for a in arrays]


def onchip(array):
    return pltpu.with_memory_space_constraint(array, pltpu.VMEM)


def offchip(array):
    return pltpu.with_memory_space_constraint(array, pltpu.HBM)


def grant(mib):
    return pltpu.CompilerParams(vmem_limit_bytes=mib << 20)


def call(body, outs, *arrays, scratch=(), stay=(), mib=12):
    arrays = [onchip(a) if k in stay else a for k, a in enumerate(arrays)]
    return pl.pallas_call(
        body,
        out_shape=outs,
        in_specs=whole(*arrays),
        out_specs=jax.tree.map(lambda _: pl.BlockSpec(memory_space=pltpu.VMEM), outs),
        scratch_shapes=list(scratch),
        compiler_params=grant(mib),
    )(*arrays)


def pack_heads(rows, owners):
    kinds, patches, width = rows.shape
    share = width // owners

    def body(rows_ref, out_ref):
        for kind in range(kinds):
            values = rows_ref[kind]
            for owner in range(owners):
                out_ref[owner, :, kind * share : (kind + 1) * share] = values[
                    :, owner * share : (owner + 1) * share
                ]

    return call(body, pltpu.HBM((owners, patches, kinds * share), rows.dtype), rows)


def vision_attention(spread, scalars):
    owners, patches, width = spread.shape
    share = width // 3
    heads = share // VIT_HDIM
    slots = owners * patches
    block = 128
    lanes = 128
    tail = share - lanes
    folds = lanes // tail
    tail_rows = patches // folds
    factor = VIT_HDIM ** (-0.5) * LOG2E

    def body(scalars_ref, spread_ref, out_ref):
        values = spread_ref[...].reshape(slots, width)
        keys = values[:, share : 2 * share]
        last = values[:, 2 * share :]
        usable = lax.broadcasted_iota(jnp.int32, (1, slots), 1) < scalars_ref[0]
        lane_head = lax.broadcasted_iota(jnp.int32, (1, share), 1) // VIT_HDIM
        for start in range(0, slots, block):
            query = values[start : start + block, :share]
            result = jnp.zeros((block, share), jnp.float32)
            for head in range(heads):
                own = lane_head == head
                picked = jnp.where(own, query, jnp.zeros_like(query))
                scores = lax.dot_general(
                    picked, keys, (((1,), (1,)), ((), ())), preferred_element_type=jnp.float32
                )
                scores = jnp.where(usable, scores, masked_score)
                peak = jnp.max(scores, axis=-1, keepdims=True)
                weights = jnp.exp2((scores - peak) * factor)
                weight_sum = jnp.sum(weights, axis=-1, keepdims=True)
                blended = jnp.dot(
                    weights.astype(jnp.bfloat16), last, preferred_element_type=jnp.float32
                )
                result = jnp.where(own, blended / weight_sum, result)
            for part in range(block // patches):
                piece = result[part * patches : (part + 1) * patches]
                owner = start // patches + part
                out_ref[owner, :patches, :] = piece[:, :lanes].astype(jnp.bfloat16)
                out_ref[owner, patches:, :] = jnp.concatenate(
                    [piece[k * tail_rows : (k + 1) * tail_rows, lanes:] for k in range(folds)], axis=1
                ).astype(jnp.bfloat16)

    out = pltpu.HBM((owners, patches + tail_rows, lanes), jnp.bfloat16)
    return call(body, out, scalars, spread, stay=(1,))


def project_norm(scalars, returned, out_weight, gain, plane, seqs, tps, rows_local):
    owners, packed_rows, lanes = returned.shape
    width = out_weight.shape[0]
    share = width // owners
    tail = share - lanes
    folds = lanes // tail
    patches = packed_rows * folds // (folds + 1)
    token_rows = patches // 4
    tiles = width // lanes

    def body(scalars_ref, returned_ref, weight_ref, gain_ref, out_ref, rows_ref):
        pieces = []
        for owner in range(owners):
            pieces.append(returned_ref[owner, :patches, :].astype(jnp.float32))
            rest = returned_ref[owner, patches:, :].astype(jnp.float32)
            pieces.append(
                jnp.concatenate([rest[:, k * tail : (k + 1) * tail] for k in range(folds)], axis=0)
            )
        attended = jnp.concatenate(pieces, axis=1).astype(jnp.bfloat16)
        hidden = jnp.dot(attended, weight_ref[...], preferred_element_type=jnp.float32)
        ids = lax.broadcasted_iota(jnp.int32, (patches, 1), 0) + scalars_ref[1]
        hidden = jnp.where(ids < scalars_ref[0], hidden, 0.0)
        centred = hidden - jnp.mean(hidden, axis=-1, keepdims=True)
        spread_sq = jnp.mean(centred * centred, axis=-1, keepdims=True)
        normed = centred * lax.rsqrt(spread_sq + 1e-06) * gain_ref[...]
        for tile in range(tiles):
            rows_ref[tile] = normed[:, tile * lanes : (tile + 1) * lanes]
        even = scalars_ref[2] == 0
        for xq in range(plane):
            pair = [
                jnp.concatenate(
                    [
                        rows_ref[tile, pl.ds(2 * xq + core, token_rows, stride=4), :]
                        for tile in range(tiles)
                    ],
                    axis=1,
                ).astype(jnp.bfloat16)
                for core in range(2)
            ]
            first = jnp.where(even, pair[0], pair[1])
            second = jnp.where(even, pair[1], pair[0])
            for sq in range(seqs):
                for tq in range(tps):
                    place = (xq * seqs + sq) * tps + tq
                    cut = slice(sq * rows_local, (sq + 1) * rows_local)
                    out_ref[place, :, :rows_local] = first[:, cut]
                    out_ref[place, :, rows_local:] = second[:, cut]

    out = pltpu.HBM((plane * seqs * tps, token_rows, 2 * rows_local), jnp.bfloat16)
    return call(
        body, out, scalars, returned, out_weight, gain[None],
        scratch=[pltpu.VMEM((tiles, patches, lanes), jnp.float32)],
        stay=(1,), mib=16,
    )


def merge_partial(scalars, tokens, own_weight, other_weight):
    quarters, half, depth = tokens.shape
    rows_local, columns = own_weight.shape
    block = 512

    def body(scalars_ref, tokens_ref, own_ref, other_ref, sent_ref, kept_ref):
        rows = jnp.concatenate([tokens_ref[scalars_ref[3 + k]] for k in range(quarters)], axis=0)
        result = jnp.dot(rows[:, :rows_local], own_ref[...], preferred_element_type=jnp.float32)
        result = result + jnp.dot(
            rows[:, rows_local:], other_ref[...], preferred_element_type=jnp.float32
        )
        sent_ref[...] = result[: 2 * half].astype(jnp.bfloat16)
        kept_ref[...] = result[2 * half :]

    weight_spec = pl.BlockSpec((rows_local, block), lambda n: (0, n))
    out_spec = pl.BlockSpec((2 * half, block), lambda n: (0, n))
    return pl.pallas_call(
        body,
        grid=(columns // block,),
        out_shape=(
            jax.ShapeDtypeStruct((2 * half, columns), jnp.bfloat16),
            jax.ShapeDtypeStruct((2 * half, columns), jnp.float32),
        ),
        in_specs=[
            pl.BlockSpec(memory_space=pltpu.SMEM),
            pl.BlockSpec((quarters, half, depth), lambda n: (0, 0, 0)),
            weight_spec,
            weight_spec,
        ],
        out_specs=(out_spec, out_spec),
        compiler_params=grant(24),
    )(scalars, onchip(tokens), offchip(own_weight), offchip(other_weight))


def add_received(kept, received):
    half = kept.shape[0] // 2

    def body(kept_ref, received_ref, sent_ref, out_ref):
        result = kept_ref[...] + received_ref[...].astype(jnp.float32)
        sent_ref[...] = result[:half].astype(jnp.bfloat16)
        out_ref[...] = result[half:]

    outs = (
        jax.ShapeDtypeStruct((half, kept.shape[1]), jnp.bfloat16),
        jax.ShapeDtypeStruct((half, kept.shape[1]), jnp.float32),
    )
    return call(body, outs, kept, received, stay=(0, 1))


def project_visual(scalars, kept, received, gain, blocks, tps):
    half, depth = kept.shape
    width = blocks[0].shape[1]
    count = len(blocks)
    extra = 16

    def body(scalars_ref, kept_ref, received_ref, gain_ref, *refs):
        block_refs, out_ref = refs[:count], refs[count]
        buffers, sems = refs[count + 1 :]
        copies = [
            pltpu.make_async_copy(block_refs[k], buffers.at[k], sems.at[k]) for k in range(count)
        ]
        for copy in copies:
            copy.start()
        embedded = kept_ref[...] + received_ref[...].astype(jnp.float32)
        squares = jnp.sum(embedded * embedded, axis=-1, keepdims=True)
        gained = (embedded * gain_ref[...]).astype(jnp.bfloat16)
        flat = jnp.broadcast_to(squares, (half, 128)).T[:extra]
        coarse = flat.astype(jnp.bfloat16).astype(jnp.float32)
        upper = lax.broadcasted_iota(jnp.int32, (extra, half), 0) < extra // 2
        both = jnp.where(upper, coarse, flat - coarse)
        both = jnp.concatenate([both, jnp.zeros((extra, width - half), jnp.float32)], axis=1)
        both = both.astype(jnp.bfloat16)
        for dest in range(tps):
            out_ref[dest, 2 * half :, :] = both
        for k in range(count):
            copies[k].wait()
            term = jnp.dot(gained, buffers[k], preferred_element_type=jnp.float32)
            row = pl.multiple_of(scalars_ref[11 + 2 * k] * half, half)
            out_ref[scalars_ref[10 + 2 * k], pl.ds(row, half), :] = term.astype(jnp.bfloat16)

    out = jax.ShapeDtypeStruct((tps, 2 * half + extra, width), jnp.bfloat16)
    return pl.pallas_call(
        body,
        out_shape=out,
        in_specs=[pl.BlockSpec(memory_space=pltpu.SMEM)]
        + [pl.BlockSpec(memory_space=pltpu.VMEM)] * 3
        + [pl.BlockSpec(memory_space=pl.ANY)] * count,
        out_specs=pl.BlockSpec(memory_space=pltpu.VMEM),
        scratch_shapes=[
            pltpu.VMEM((count, depth, width), jnp.bfloat16),
            pltpu.SemaphoreType.DMA((count,)),
        ],
        compiler_params=grant(24),
    )(scalars, onchip(kept), onchip(received), gain[None], *[offchip(block) for block in blocks])


def finish_visual(sums, half):
    width = sums.shape[2]

    def body(sums_ref, out_ref):
        total = jnp.sum(sums_ref[...].astype(jnp.float32), axis=0)
        flat = total[2 * half : 2 * half + 8] + total[2 * half + 8 :]
        squares = jnp.broadcast_to(flat[:1, :128], (128, 128)).T[:half, :1]
        scale = lax.rsqrt(squares / D + 1e-06)
        out_ref[:half] = (total[:half] * scale).astype(jnp.bfloat16)
        out_ref[half:] = (total[half : 2 * half] * scale).astype(jnp.bfloat16)

    return call(body, jax.ShapeDtypeStruct((2 * half, width), jnp.bfloat16), sums, stay=(0,))


def split_queries(block, kv_local):
    tokens, heads, width = block.shape
    groups = heads // kv_local
    wide = block.astype(jnp.float32).reshape(tokens, kv_local, groups, width)
    return [
        wide[:, k].reshape(tokens * groups, width).astype(jnp.bfloat16) for k in range(kv_local)
    ]


def prompt_own(queries, span_kv, kv_head):
    tokens, heads, width = queries.shape
    kv_local = span_kv.shape[2]
    groups = heads // kv_local
    block = 128
    rows = block * groups
    factor = HD ** (-0.5) * LOG2E

    def body(queries_ref, span_ref, out_ref, stats_ref):
        every_key = span_ref[:, 0, kv_head, :]
        every_value = span_ref[:, 1, kv_head, :]
        for index in range(tokens // block):
            start = index * block
            query = split_queries(queries_ref[start : start + block], kv_local)[kv_head]
            extent = start + block
            keys = every_key[:extent]
            values = every_value[:extent]
            scores = lax.dot_general(
                keys, query, (((1,), (1,)), ((), ())), preferred_element_type=jnp.float32
            )
            key_ids = lax.broadcasted_iota(jnp.int32, (extent, rows), 0)
            token_ids = start + lax.broadcasted_iota(jnp.int32, (extent, rows), 1) // groups
            scores = jnp.where(key_ids <= token_ids, scores, masked_score)
            peak = jnp.max(scores, axis=0, keepdims=True)
            weights = jnp.exp2((scores - peak) * factor)
            cut = slice(start * groups, extent * groups)
            stats_ref[0:1, cut] = peak
            stats_ref[1:2, cut] = jnp.sum(weights, axis=0, keepdims=True)
            out_ref[:, cut] = lax.dot_general(
                values, weights.astype(jnp.bfloat16), (((0,), (0,)), ((), ())),
                preferred_element_type=jnp.float32,
            )

    outs = (
        pltpu.HBM((width, tokens * groups), jnp.float32),
        pltpu.HBM((2, tokens * groups), jnp.float32),
    )
    return call(body, outs, offchip(queries), offchip(span_kv), mib=24)


def prompt_visual(scalars, queries, own, twin, near, half):
    tokens, heads, width = queries.shape
    kv_local = len(near)
    groups = heads // kv_local
    block = 128
    rows = block * groups
    factor = HD ** (-0.5) * LOG2E

    def body(scalars_ref, queries_ref, own_ref, twin_ref, *refs):
        near_refs, out_ref = refs[:-1], refs[-1]
        split = split_queries(queries_ref[...], kv_local)
        ids = lax.broadcasted_iota(jnp.int32, (2 * half, 1), 0)
        ids = jnp.where(ids < half, ids + scalars_ref[8], ids - half + scalars_ref[9])
        seen = ids < scalars_ref[7]
        results = []
        for k in range(kv_local):
            cut = slice(k * width, (k + 1) * width)
            keys = jnp.concatenate([own_ref[:half, cut], twin_ref[:half, cut]], axis=0)
            values = jnp.concatenate([own_ref[half:, cut], twin_ref[half:, cut]], axis=0)
            scores = lax.dot_general(
                keys, split[k], (((1,), (1,)), ((), ())), preferred_element_type=jnp.float32
            )
            scores = jnp.where(seen, scores, masked_score)
            stats = near_refs[2 * k + 1][...]
            peak = jnp.maximum(stats[0:1], jnp.max(scores, axis=0, keepdims=True))
            weights = jnp.exp2((scores - peak) * factor)
            decay = jnp.exp2((stats[0:1] - peak) * factor)
            total = stats[1:2] * decay + jnp.sum(weights, axis=0, keepdims=True)
            blended = lax.dot_general(
                values, weights.astype(jnp.bfloat16), (((0,), (0,)), ((), ())),
                preferred_element_type=jnp.float32,
            )
            blended = (blended + near_refs[2 * k][...] * decay) / total
            results.append(blended.T.reshape(block, 1, groups, width))
        joined = jnp.concatenate(results, axis=1).reshape(block, heads, width)
        out_ref[...] = joined.astype(jnp.bfloat16)

    query_spec = pl.BlockSpec((block, heads, width), lambda n: (n, 0, 0))
    fixed = pl.BlockSpec((2 * half, kv_local * width), lambda n: (0, 0))
    near_specs = [
        pl.BlockSpec((width, rows), lambda n: (0, n)),
        pl.BlockSpec((2, rows), lambda n: (0, n)),
    ] * kv_local
    return pl.pallas_call(
        body,
        grid=(tokens // block,),
        out_shape=jax.ShapeDtypeStruct(queries.shape, jnp.bfloat16),
        in_specs=[pl.BlockSpec(memory_space=pltpu.SMEM), query_spec, fixed, fixed] + near_specs,
        out_specs=query_spec,
        compiler_params=grant(24),
    )(scalars, offchip(queries), onchip(own), onchip(twin), *[offchip(part) for pair in near for part in pair])


def swap_pairs(plane, seqs, tps, move):
    pairs = []
    for x in range(plane):
        for c in range(2):
            for s in range(seqs):
                for t in range(tps):
                    x2, c2, s2 = move(x, c, s)
                    pairs.append((((x * 2 + c) * seqs + s) * tps + t, ((x2 * 2 + c2) * seqs + s2) * tps + t))
    return pairs


def fast_local(
    vit_qkv,
    patch_counts,
    vit_out_weight,
    vit_norm_gain,
    merger_weight,
    lm_norm_gain,
    kv_weight,
    queries,
    span_kv,
):
    everything = ("x", "c", "seq", "tp")
    plane = lax.axis_size("x")
    seqs = lax.axis_size("seq")
    tps = lax.axis_size("tp")
    x, c, s, t = (lax.axis_index(name) for name in everything)
    owners = seqs * tps
    patch_rows = vit_qkv.shape[1]
    token_rows = patch_rows // 4
    half = tps * token_rows
    rows_local = merger_weight.shape[0]
    patch_total = patch_counts[0]

    def swap(value, move):
        return lax.ppermute(value, everything, swap_pairs(plane, seqs, tps, move))

    def exchange(value, names):
        return lax.all_to_all(value, names, split_axis=0, concat_axis=0, tiled=True)

    def other_core(x, c, s):
        return x, 1 - c, s

    def first_hop(x, c, s):
        return (1 - x, c, s) if c == 0 else (x, c, 1 - s)

    def second_hop(x, c, s):
        return (x, c, 1 - s) if c == 0 else (1 - x, c, s)

    def other_seq(x, c, s):
        return x, c, 1 - s

    def quarter(xq, sq):
        return xq * seqs + sq

    even = c == 0
    scalars = [patch_total, (s * tps + t) * patch_rows, c, quarter(1 - x, 1 - s)]
    scalars.append(jnp.where(even, quarter(1 - x, s), quarter(x, 1 - s)))
    scalars.append(jnp.where(even, quarter(x, 1 - s), quarter(1 - x, s)))
    scalars += [quarter(x, s), patch_total // 4, s * half, (1 - s) * half]
    for core_step in range(2):
        owner = c ^ core_step
        for far_step in range(2):
            for hop_step in range(2):
                owner_seq = s ^ jnp.where(owner == 0, far_step, hop_step)
                scalars += [owner * seqs + owner_seq, x ^ jnp.where(owner == 0, hop_step, far_step)]
    scalars = jnp.stack(scalars).astype(jnp.int32)

    other_rows = swap(merger_weight, other_core)
    packed = pack_heads(jnp.transpose(vit_qkv[0], (1, 0, 2)), owners)
    spread = exchange(packed, ("seq", "tp"))

    near_block = swap(kv_weight, first_hop)
    side_block = swap(kv_weight, second_hop)
    far_block = swap(near_block, second_hop)
    chip_blocks = [kv_weight, near_block, side_block, far_block]
    kv_blocks = list(chip_blocks)
    for block in chip_blocks:
        kv_blocks.append(swap(block, other_core))

    near = []
    for k in range(span_kv.shape[3]):
        near.append(prompt_own(queries[0], span_kv[0], k))

    attended = vision_attention(spread, scalars)
    returned = exchange(attended, ("seq", "tp"))
    merged = project_norm(
        scalars, returned, vit_out_weight, vit_norm_gain, plane, seqs, tps, rows_local
    )

    tokens = exchange(merged, ("x", "seq", "tp")).reshape(plane * seqs, half, 2 * rows_local)
    sent, kept = merge_partial(scalars, tokens, merger_weight, other_rows)
    received = swap(sent, first_hop)
    sent, kept = add_received(kept, received)
    received = swap(sent, second_hop)

    payload = project_visual(scalars, kept, received, lm_norm_gain, kv_blocks, tps)
    sums = exchange(payload, "tp")
    visual = finish_visual(sums, half)
    twin = swap(visual, other_seq)

    return prompt_visual(scalars, queries[0], visual, twin, near, half)[None]


def solution(mesh):
    sizes = dict(mesh.shape)
    images, seqs, tps = (sizes[name] for name in ("img", "seq", "tp"))
    suited = (
        images == 4
        and seqs == 2
        and images * seqs == 2 * tps
        and VIT_HEADS % (seqs * tps) == 0
        and KVH % tps == 0
    )
    if not suited:
        placed = (
            P("img", ("seq", "tp"), None, None),
            P("img"),
            P(),
            P(),
            P(("img", "seq"), "tp"),
            P("tp"),
            P("tp", ("img", "seq")),
            P("img", "seq", "tp", None),
            P("img", "seq", None, "tp", None),
        )
        return jax.shard_map(
            local, mesh=mesh, in_specs=placed, out_specs=P("img", "seq", "tp", None), check_vma=False
        )
    split = Mesh(
        mesh.devices.reshape(images // 2, 2, seqs, tps), ("x", "c", "seq", "tp")
    )
    image = ("x", "c")
    placed = (
        P(image, ("seq", "tp"), None, None),
        P(image),
        P(),
        P(),
        P(("x", "c", "seq"), "tp"),
        P("tp"),
        P("tp", ("x", "c", "seq")),
        P(image, "seq", "tp", None),
        P(image, "seq", None, "tp", None),
    )

    return jax.shard_map(
        fast_local, mesh=split, in_specs=placed, out_specs=P(image, "seq", "tp", None), check_vma=False
    )
```
